256 devices in a mesh: space: 16 (over z, core), tracer: 4 (over x), month: 4 (over y).
Axes of the slice: x: 4, y: 4, z: 8, core: 2. Of those that a mesh axis runs over, the one named last changes fastest.
Arguments:
- state: float32 [32, 16, 128, 512], P('tracer', 'month', 'space'), may hold values from -20 to 20
- coefficients: bfloat16 [4, 27, 16, 128, 512], P('month', None, None, 'space'), may hold values from 0 to 1, as said below
- rates: float32 [32], P('tracer'), may hold values from 0.05 to 0.5
- land_mask: int32 [128, 512], P('space'), may hold values 0 or 1
- wet_levels: int32 [128, 512], P('space'), may hold values from 1 to 16
- basis: float32 [4, 32, 16, 128, 512], P(None, 'tracer', 'month', 'space'), may hold values from -20 to 20
Outputs:
- residual: float32 [32, 16, 128, 512], P('tracer', 'month', 'space')
- next_basis: float32 [32, 16, 128, 512], P('tracer', 'month', 'space')
- krylov: float32 [6], replicated
The draws below stay inside these ranges and needn't reach their ends.
Inputs may be any that keep to these rules, and one draw needn't show every extreme that they name: `coefficients`: the 27 weights of a cell in a month are non-negative and sum to one.
All inputs are finite; a program needn't handle non-finite values. No bound on the sum of `land_mask` on one device may be relied on, other than what follows from the above.
Results may differ from the reference program's by a relative error of at most 0.0011.
Values may be sent and summed in bfloat16 or wider, within the bound.
No kernel may reach another device: no remote copies, remote signals or barrier semaphores. Data moves between devices by JAX's collectives and lax.ppermute only.
A program may use at most 64 MiB of HBM per device.

```python
import math
import jax
import jax.numpy as jnp
from jax import lax

TRACERS = 32
LAT = 512
STEPS = 4
BASIS = 4
LON = 128
LEV = 16


def linear_ramp(length):
    return jnp.arange(length, dtype=jnp.float32) / max(length - 1, 1) - 0.5


def profile(seed_key):
    tracer_gain = 2.0 ** jax.random.uniform(seed_key, (TRACERS,), jnp.float32, -0.5, 0.5)
    tracer_part = 3.0 ** linear_ramp(TRACERS) * tracer_gain
    level_part = 3.0 ** linear_ramp(LEV)
    column_part = 3.0 ** linear_ramp(LON)
    return tracer_part[:, None, None, None] * level_part[None, :, None, None] * column_part[None, None, :, None]


def draw_state(key, part):
    seeds = jax.random.split(jax.random.fold_in(key, 3), 2)
    amplitude = profile(seeds[0])
    grid_shape = (TRACERS, LEV, LON, LAT)
    jitter = jax.random.normal(seeds[1], grid_shape, jnp.float32)
    return jnp.clip(amplitude * jitter, -20.0, 20.0)


def draw_basis(key, part):
    seeds = jax.random.split(jax.random.fold_in(key, 5), 3)
    amplitude = profile(seeds[0])
    grid_shape = (TRACERS, LEV, LON, LAT)
    common = jax.random.normal(seeds[1], grid_shape, jnp.float32)
    jitter = jax.random.normal(seeds[2], (BASIS,) + grid_shape, jnp.float32)
    mixture = 0.6 * common[None] + 0.8 * jitter
    return jnp.clip(amplitude[None] * mixture, -20.0, 20.0)


def draw_coefficients(key, part):
    grid_shape = (STEPS, 27, LEV, LON, LAT)
    folded = jax.random.fold_in(key, 7)
    neighbour_weight = jax.random.uniform(folded, grid_shape, jnp.float32, 0.1, 1.0) * (0.95 / 26.0)
    centre = (jnp.arange(27) == 13)[None, :, None, None, None]
    neighbour_weight = jnp.where(centre, 0.0, neighbour_weight)
    centre_weight = 1.0 - jnp.sum(neighbour_weight, axis=1, keepdims=True)
    return jnp.where(centre, centre_weight, neighbour_weight).astype(jnp.bfloat16)


def with_ends(array, own_key, smallest, top_value):
    place = [jax.random.randint(jax.random.fold_in(own_key, axis), (), 0, length) for axis, length in enumerate(array.shape)]
    main_axis = array.shape.index(max(array.shape))
    next_to = place[:main_axis] + [(place[main_axis] + 1) % array.shape[main_axis]] + place[main_axis + 1:]
    return array.at[tuple(place)].set(smallest).at[tuple(next_to)].set(top_value)


def steps_of(stream_key, extent, cuts, low, high):
    level = 1.0
    for position, blocks in cuts:
        steps = jax.random.uniform(jax.random.fold_in(jax.random.fold_in(stream_key, 6), position), (blocks,), jnp.float32, low / len(cuts), high / len(cuts))
        level = level * jnp.repeat(jnp.exp(steps), extent[position] // blocks).reshape((-1,) + (1,) * (len(extent) - 1 - position))
    return level


def setup_inputs(seed: int = 0) -> dict:
    splits = jax.random.split(jax.random.key(seed), 7)
    return {
        "state": draw_state(jax.random.fold_in(splits[6], 71), 0),
        "coefficients": draw_coefficients(jax.random.fold_in(splits[6], 71), 0),
        "rates": jnp.clip(jnp.exp(math.log(0.5) - 2.3025851 * jax.random.uniform(splits[2], (TRACERS,), jnp.float32) ** steps_of(splits[2], (TRACERS,), ((0, 4),), -0.2, 0.2)), 0.05, 0.5),
        "land_mask": with_ends((jax.random.randint(splits[3], (LON, LAT), 0, 4) < 3).astype(jnp.int32), jax.random.fold_in(splits[3], 1), 0, 1),
        "wet_levels": with_ends(jax.random.randint(splits[4], (LON, LAT), 1, LEV + 1), jax.random.fold_in(splits[4], 1), 1, LEV).astype(jnp.int32),
        "basis": draw_basis(jax.random.fold_in(splits[6], 71), 0),
    }


def apply_stencil(padded, weights, grid_shape):
    levels, columns, lat_rows = grid_shape
    summed = jnp.zeros(padded.shape[:-3] + grid_shape, jnp.float32)
    for depth_shift in range(3):
        for across in range(3):
            for along_shift in range(3):
                weight = weights[depth_shift * 9 + across * 3 + along_shift].astype(jnp.float32)
                summed = summed + weight * padded[..., depth_shift:depth_shift + levels, across:across + columns, along_shift:along_shift + lat_rows]
    return summed

def reference(state, coefficients, rates, land_mask, wet_levels, basis):
    grid_shape = (LEV, LON, LAT)
    level_index = jnp.arange(LEV, dtype=jnp.int32)
    wet_cells = jnp.where((land_mask[None] == 1) & (level_index[:, None, None] < wet_levels[None]), 1.0, 0.0).astype(jnp.float32)
    uptake = rates[:, None, None, None]
    concentration = state * wet_cells
    tangent = basis[BASIS - 1] * wet_cells
    for month_step in range(STEPS):
        paired = jnp.stack([concentration, tangent])
        padded = jnp.pad(paired, ((0, 0), (0, 0), (1, 1), (1, 1), (1, 1)))
        transported = apply_stencil(padded, coefficients[month_step], grid_shape)
        square = concentration * concentration
        denominator = 1.0 + square
        new_concentration = wet_cells * (transported[0] - uptake * concentration * square / denominator)
        tangent = wet_cells * (transported[1] - uptake * square * (3.0 + square) / (denominator * denominator) * tangent)
        concentration = new_concentration
    residual = concentration - state
    jacobian_product = tangent - basis[BASIS - 1]
    cell_count = float(TRACERS * LEV * LON * LAT)
    projected = lax.optimization_barrier(jnp.sum(basis * jacobian_product[None], axis=(1, 2, 3, 4))) / cell_count
    remainder = jacobian_product - lax.optimization_barrier(jnp.sum(projected[:, None, None, None, None] * basis, axis=0))
    norm_scale = jnp.sqrt(jnp.sum(remainder * remainder) / cell_count + 1e-06)
    next_basis = remainder / norm_scale
    residual_rms = jnp.sqrt(jnp.sum(residual * residual) / cell_count + 1e-06)
    krylov = jnp.concatenate([projected, jnp.stack([norm_scale, residual_rms])])
    return (residual, next_basis, krylov)
```

```python
import jax
import jax.numpy as jnp
from jax import lax
from jax.sharding import PartitionSpec as P


def padded_2(x, sides, width):
    for axis, dim in sides:
        size, length = (lax.axis_size(axis), x.shape[dim])
        up = [(i, (i + 1) % size) for i in range(size - 1)]
        down = [(j, i) for i, j in up]
        last = lax.slice_in_dim(x, length - width, length, axis=dim)
        initial = lax.slice_in_dim(x, 0, width, axis=dim)
        before = lax.ppermute(last, axis, up)
        after = lax.ppermute(initial, axis, down)
        x = jnp.concatenate([before, x, after], axis=dim)
    return x


def apply_stencil(padded, weights, grid_shape):
    levels, columns, lat_rows = grid_shape
    summed = jnp.zeros(padded.shape[:-3] + grid_shape, jnp.float32)
    for depth_shift in range(3):
        for across in range(3):
            for along_shift in range(3):
                weight = weights[depth_shift * 9 + across * 3 + along_shift].astype(jnp.float32)
                summed = (
                    summed
                    + weight
                    * padded[
                        ...,
                        depth_shift : depth_shift + levels,
                        across : across + columns,
                        along_shift : along_shift + lat_rows,
                    ]
                )
    return summed


def spread_sum(values, axes):
    count = lax.axis_size(axes)
    rows = jnp.broadcast_to(values[None], (count,) + values.shape)
    return jnp.sum(lax.all_to_all(rows, axes, 0, 0, tiled=True), axis=0)


def sum_everywhere(values):
    row = jnp.zeros((1, 128), jnp.float32).at[0, : values.shape[0]].set(values)
    row = spread_sum(row, ("tracer", "month"))
    return spread_sum(row, ("space",))[0, : values.shape[0]]


def on_device(state, coefficients, rates, land_mask, wet_levels, basis):
    tracers_here, levels_here, columns_here, rows_here = state.shape
    grid_shape = (levels_here, columns_here, rows_here)
    level_start = lax.axis_index("month") * levels_here
    level_index = level_start + jnp.arange(levels_here, dtype=jnp.int32)
    wet_cells = jnp.where(
        (land_mask[None] == 1) & (level_index[:, None, None] < wet_levels[None]), 1.0, 0.0
    ).astype(jnp.float32)
    uptake = rates[:, None, None, None]
    months_here = coefficients.shape[0]
    own_months = lax.all_to_all(coefficients, "month", split_axis=2, concat_axis=0, tiled=True)
    concentration = state * wet_cells
    tangent = basis[-1] * wet_cells
    for month_step in range(months_here * lax.axis_size("month")):
        weights = own_months[month_step]
        paired = jnp.stack([concentration, tangent])
        margins = padded_2(paired.astype(jnp.bfloat16), (("space", 3), ("month", 2)), 1).astype(
            paired.dtype
        )
        margins = jnp.pad(margins, ((0, 0), (0, 0), (0, 0), (0, 0), (1, 1)))
        transported = apply_stencil(margins, weights, grid_shape)
        square = concentration * concentration
        denominator = 1.0 + square
        new_concentration = wet_cells * (
            transported[0] - uptake * concentration * square / denominator
        )
        tangent = wet_cells * (
            transported[1]
            - uptake * square * (3.0 + square) / (denominator * denominator) * tangent
        )
        concentration = new_concentration
    residual = concentration - state
    jacobian_product = tangent - basis[-1]
    cell_count = float(
        state.size * lax.axis_size("space") * lax.axis_size("tracer") * lax.axis_size("month")
    )
    pairs = [(k, m) for k in range(4) for m in range(k, 4)]
    parts = [jnp.sum(basis[k] * jacobian_product) for k in range(4)]
    parts += [jnp.sum(jacobian_product * jacobian_product), jnp.sum(residual * residual)]
    parts += [jnp.sum(basis[k] * basis[m]) for k, m in pairs]
    means = sum_everywhere(jnp.stack(parts)) / cell_count
    projected = means[:4]
    gram_term = jnp.float32(0.0)
    for place, (k, m) in enumerate(pairs):
        gram_term += (1.0 if k == m else 2.0) * projected[k] * projected[m] * means[6 + place]
    cross = 2.0 * jnp.sum(projected * projected)
    remainder = jacobian_product - jnp.sum(projected[:, None, None, None, None] * basis, axis=0)
    expanded = means[4] - cross + gram_term
    remainder_mean = lax.cond(
        expanded > 0.01 * (means[4] + cross + gram_term),
        lambda r: expanded,
        lambda r: sum_everywhere(jnp.sum(r * r)[None])[0] / cell_count,
        remainder,
    )
    norm_scale = jnp.sqrt(remainder_mean + 1e-06)
    next_basis = remainder / norm_scale
    residual_rms = jnp.sqrt(means[5] + 1e-06)
    krylov = jnp.concatenate([projected, jnp.stack([norm_scale, residual_rms])])
    return (residual, next_basis, krylov)


def solution(mesh):
    return jax.shard_map(
        on_device,
        mesh=mesh,
        in_specs=(
            P("tracer", "month", "space", None),
            P("month", None, None, "space", None),
            P("tracer"),
            P("space", None),
            P("space", None),
            P(None, "tracer", "month", "space", None),
        ),
        out_specs=(P("tracer", "month", "space", None), P("tracer", "month", "space", None), P()),
        check_vma=False,
    )
```

```python
import functools

import jax
import jax.numpy as jnp
from jax import lax
from jax.experimental import pallas as pl
from jax.experimental.pallas import tpu as pltpu
from jax.sharding import PartitionSpec as P

F32 = jnp.float32
BF16 = jnp.bfloat16
TAPS = [(dl, di) for dl in (-1, 0, 1) for di in (-1, 0, 1)]


VMEM_LIMIT = 20 * 2**20


def call(body, outs, cost, scratch=(), in_specs=None):
    return pl.pallas_call(
        body,
        out_shape=[jax.ShapeDtypeStruct(s, d) for s, d in outs],
        scratch_shapes=list(scratch),
        cost_estimate=pl.CostEstimate(flops=cost, transcendentals=0, bytes_accessed=cost // 8),
        compiler_params=pltpu.CompilerParams(vmem_limit_bytes=VMEM_LIMIT),
        **({} if in_specs is None else {"in_specs": in_specs}),
    )


def reader(levels, columns, inner_ref, outer_ref, sides_ref):
    def get(f, l, i):
        if i in (0, columns - 1):
            return sides_ref[f, l, int(i > 0)]
        if l in (0, levels - 1):
            return outer_ref[f, int(l > 0), i]
        return inner_ref[f, l - 1, i]

    return get


def init_body(levels, columns, start_ref, rates_ref, land_ref, depth_ref, state_ref, basis_ref, *outs):
    inner_ref, outer_ref, sides_ref, wet_ref, rate_ref, lev_lo, lev_hi, lon_lo, lon_hi, last_ref, sem = outs
    fetch = pltpu.make_async_copy(basis_ref.at[basis_ref.shape[0] - 1], last_ref, sem)
    fetch.start()
    tracer = lax.broadcasted_iota(jnp.int32, rate_ref.shape, 0)
    rate = jnp.zeros(rate_ref.shape, F32)
    for n in range(rate_ref.shape[0]):
        rate = jnp.where(tracer == n, rates_ref[n], rate)
    rate_ref[...] = rate
    for l in range(levels):
        ocean = (land_ref[...] == 1) & (start_ref[0] + l < depth_ref[...])
        wet_ref[l] = jnp.where(ocean, 1.0, 0.0).astype(F32)
    for f, ref in enumerate((state_ref, last_ref)):
        if f:
            fetch.wait()
        for l in range(levels):
            rows = pltpu.einshape("tix->itx", ref[:, l])
            for i in range(columns):
                row = rows[i] * wet_ref[l, pl.ds(i, 1), :]
                short = row.astype(BF16)
                if i in (0, columns - 1):
                    sides_ref[f, l, int(i > 0)] = row
                    (lon_hi if i else lon_lo)[f, l] = short
                elif l in (0, levels - 1):
                    outer_ref[f, int(l > 0), i] = row
                else:
                    inner_ref[f, l - 1, i] = row
                if l in (0, levels - 1):
                    (lev_hi if l else lev_lo)[f, i] = short


def combine(sums):
    n = sums[1].shape[1]
    return sums[1] + pltpu.roll(sums[2], n - 1, 1) + pltpu.roll(sums[0], 1, 1)


def tap_sums(taps):
    acc = [[None] * 3, [None] * 3]
    for weights, rows in taps:
        for dj in range(3):
            for f in range(2):
                term = weights[dj] * rows[f]
                acc[f][dj] = term if acc[f][dj] is None else acc[f][dj] + term
    return combine(acc[0]), combine(acc[1])


def prepare_body(w_refs, wf_ref):
    index_ref, *parts = w_refs
    size = parts[0].shape[3]
    taps, levels, columns, lat = wf_ref.shape
    for n, ref in enumerate(parts):
        place = lax.rem(index_ref[0] - n + len(parts), len(parts))
        lanes = pl.ds(pl.multiple_of(place * size, size), size)

        def spread_part(k, carry, ref=ref, lanes=lanes):
            for l in range(levels):
                wf_ref[k, l, :, lanes] = ref[k, l].astype(F32)
            return carry

        lax.fori_loop(0, taps, spread_part, 0, unroll=3)
    lane = lax.broadcasted_iota(jnp.int32, (columns, lat), 1)

    def move(k, carry):
        for l in range(levels):
            wf_ref[3 * k + 2, l] = jnp.where(lane == 0, 0.0, pltpu.roll(wf_ref[3 * k + 2, l], 1, 1))
            wf_ref[3 * k, l] = jnp.where(lane == lat - 1, 0.0, pltpu.roll(wf_ref[3 * k, l], lat - 1, 1))
        return carry

    lax.fori_loop(0, taps // 3, move, 0, unroll=3)


def part_body(levels, columns, mine, outer, wf_ref, inner_ref, outer_ref, sides_ref, rate_ref, wet_ref, *rest):
    if outer:
        below_ref, above_ref, out_ref = rest
    else:
        (out_ref,) = rest
    get = reader(levels, columns, inner_ref, outer_ref, sides_ref)
    rate = rate_ref[...]

    def rows_at(l, i):
        if l < 0:
            return [below_ref[f, i].astype(F32) for f in range(2)]
        if l >= levels:
            return [above_ref[f, i].astype(F32) for f in range(2)]
        return [get(f, l, i) for f in range(2)]

    for n, l in enumerate(mine):
        for i in range(columns):
            taps = []
            for dl, di in TAPS:
                if 0 <= i + di < columns:
                    first = 9 * (dl + 1) + 3 * (di + 1)
                    weights = [wf_ref[first + dj, l, pl.ds(i, 1), :] for dj in range(3)]
                    taps.append((weights, rows_at(l + dl, i + di)))
            ac, at = tap_sums(taps)
            c, t = rows_at(l, i)
            square = c * c
            inverse = 1.0 / (1.0 + square)
            part = rate * square * inverse
            ac = ac - part * c
            at = at - part * inverse * (3.0 + square) * t
            if 0 < i < columns - 1:
                wet = wet_ref[l, pl.ds(i, 1), :]
                ac, at = ac * wet, at * wet
            out_ref[0, n, i] = ac
            out_ref[1, n, i] = at


def side_rows(levels, columns, inner_ref, outer_ref, wf_ref, left_ref, right_ref, wet_ref):
    for l in range(levels):
        edge = l in (0, levels - 1)
        n = int(l > 0) if edge else l - 1
        own = outer_ref if edge else inner_ref
        for side, i in ((0, 0), (1, columns - 1)):
            halo = (left_ref, right_ref)[side]
            taps = []
            for d in range(3):
                weights = [wf_ref[9 * d + 6 * side + dj, l, pl.ds(i, 1), :] for dj in range(3)]
                taps.append((weights, [halo[f, l + d].astype(F32) for f in range(2)]))
            sums = tap_sums(taps)
            wet = wet_ref[l, pl.ds(i, 1), :]
            yield l, side, i, [(own[f, n, i] + sums[f]) * wet for f in range(2)]


def side_body(levels, columns, *refs):
    sides_ref, lev_lo, lev_hi, lon_lo, lon_hi = refs[6:]
    outer_ref = refs[1]
    for l, side, i, rows in side_rows(levels, columns, *refs[:6]):
        for f in range(2):
            short = rows[f].astype(BF16)
            sides_ref[f, l, side] = rows[f]
            (lon_hi if side else lon_lo)[f, l] = short
            if l in (0, levels - 1):
                (lev_hi if l else lev_lo)[f, i] = short
    for f in range(2):
        for i in range(1, columns - 1):
            lev_lo[f, i] = outer_ref[f, 0, i].astype(BF16)
            lev_hi[f, i] = outer_ref[f, 1, i].astype(BF16)


def pack_body(columns, after_ref, below_ref, above_ref, lo_ref, hi_ref, left_out, right_out):
    levels = lo_ref.shape[1]
    for out, own, i in ((left_out, lo_ref, 0), (right_out, hi_ref, columns - 1)):
        for f in range(2):
            out[f, 0] = below_ref[f, i]
            out[f, levels + 1] = above_ref[f, i]
            for l in range(levels):
                out[f, l + 1] = own[f, l]


def lanes_of(values, first):
    lane = lax.broadcasted_iota(jnp.int32, (1, 128), 1)
    total = jnp.zeros((1, 128), F32)
    for n, v in enumerate(values):
        total = jnp.where(lane == first + n, v, total)
    return total


def gram_body(basis_ref, out_ref):
    count = basis_ref.shape[0]
    pairs = [(k, m) for k in range(count) for m in range(k, count)]

    def step(n, acc):
        rows = pl.ds(pl.multiple_of(n * 8, 8), 8)
        b = [basis_ref[k, rows, :] for k in range(count)]
        return tuple(a + b[k] * b[m] for a, (k, m) in zip(acc, pairs))

    zero = jnp.zeros((8, basis_ref.shape[2]), F32)
    acc = lax.fori_loop(0, basis_ref.shape[1] // 8, step, (zero,) * len(pairs))
    out_ref[...] = lanes_of([jnp.sum(a) for a in acc], 6)


def last_body(levels, columns, *refs):
    state_ref, basis_ref, gram_ref, res_ref, prod_ref, out_ref = refs[6:12]
    fields = refs[12:]
    inner_ref, outer_ref = refs[:2]
    sides = {}
    for l, side, i, rows in side_rows(levels, columns, *refs[:6]):
        sides[l, i] = rows
    for l in range(levels):
        for f in range(2):
            own = [sides[l, i][f] if i in (0, columns - 1)
                   else outer_ref[f, int(l > 0), i] if l in (0, levels - 1) else inner_ref[f, l - 1, i]
                   for i in range(columns)]
            fields[f][:, l] = pltpu.einshape("itx->tix", jnp.stack(own))
    count = basis_ref.shape[0]

    def step(n, acc):
        for l in range(levels):
            b = [basis_ref[k, n, l] for k in range(count)]
            residual = fields[0][n, l] - state_ref[n, l]
            product = fields[1][n, l] - b[count - 1]
            res_ref[n, l] = residual
            prod_ref[n, l] = product
            terms = [x * product for x in b] + [product * product, residual * residual]
            acc = tuple(a + x for a, x in zip(acc, terms))
        return acc

    zero = jnp.zeros(fields[0].shape[2:], F32)
    acc = lax.fori_loop(0, fields[0].shape[0], step, (zero,) * (count + 2))
    row = gram_ref[...] + lanes_of([jnp.sum(a) for a in acc], 0)
    for n in range(out_ref.shape[0]):
        out_ref[n] = row


def finish_body(cells, rows_ref, prod_ref, basis_ref, rem_ref, next_ref, krylov_ref, sure_ref):
    count = basis_ref.shape[0]
    means = rows_ref[0]
    for n in range(1, rows_ref.shape[0]):
        means = means + rows_ref[n]
    means = means / cells
    lane = lax.broadcasted_iota(jnp.int32, (1, 128), 1)

    def pick(n):
        return jnp.sum(jnp.where(lane == n, means, 0.0), axis=1, keepdims=True)

    coef = [pick(k) for k in range(count)]
    cross = sum(2.0 * c * c for c in coef)
    gram = 0.0
    place = count + 2
    for k in range(count):
        for m in range(k, count):
            gram = gram + (1.0 if k == m else 2.0) * coef[k] * coef[m] * pick(place)
            place += 1
    square = pick(count)
    expanded = square - cross + gram
    sure = jnp.where(expanded > 0.01 * (square + cross + gram), 1.0, 0.0)
    norm = jnp.sqrt(jnp.maximum(expanded, 0.0) + 1e-06)
    rms = jnp.sqrt(pick(count + 1) + 1e-06)
    krylov = jnp.where(lane == count, norm, jnp.where(lane == count + 1, rms, means))
    krylov_ref[...] = krylov[:, : count + 2]
    sure_ref[...] = sure
    inverse = 1.0 / norm

    def step(n, carry):
        rows = pl.ds(pl.multiple_of(n * 8, 8), 8)
        rem = coef[0] * basis_ref[0, rows, :]
        for k in range(1, count):
            rem = rem + coef[k] * basis_ref[k, rows, :]
        rem = prod_ref[rows, :] - rem
        rem_ref[rows, :] = rem
        next_ref[rows, :] = rem * inverse
        return carry

    lax.fori_loop(0, prod_ref.shape[0] // 8, step, 0)


def spread(x, axes):
    return lax.all_to_all(x, axes, 0, 0, tiled=True)


def copies(x, count):
    return jnp.broadcast_to(x[None], (count,) + x.shape)


def shifted(x, axis, by, wrap=False):
    size = lax.axis_size(axis)
    pairs = [(n, (n + by) % size) for n in range(size) if wrap or 0 <= n + by < size]
    return lax.ppermute(x, axis, pairs)


def after(x, *others):
    return lax.optimization_barrier((x, *others))[0]


def month_parts(coefficients, levels):
    taps, all_levels, columns, lat = coefficients.shape[1:]
    n_tracer, n_month = lax.axis_size("tracer"), lax.axis_size("month")
    part = lat // n_tracer
    me = lax.axis_index("month")
    place = lax.axis_index("tracer") * part
    found = []
    for k in range(n_month):
        level = lax.rem(me + k, n_month) * levels
        own = lax.dynamic_slice(coefficients[0], (0, level, 0, place), (taps, levels, columns, part))
        found.append(shifted(own, "month", k, True) if k else own)
    return [lax.select_n(lax.rem(me - m + n_month, n_month), *found) for m in range(n_month)]


def on_device(state, coefficients, rates, land_mask, wet_levels, basis):
    tracers, levels, columns, lat = state.shape
    count = basis.shape[0]
    n_space, n_month, n_tracer = lax.axis_size("space"), lax.axis_size("month"), lax.axis_size("tracer")
    flat = (tracers * levels * columns, lat)
    basis_rows = basis.reshape((count,) + flat)
    parts = month_parts(coefficients, levels)

    row = (tracers, lat)
    inner, outer = (2, levels - 2, columns) + row, (2, 2, columns) + row
    sides, lev, lon = (2, levels, 2) + row, (2, columns) + row, (2, levels) + row
    messages = [(lev, BF16)] * 2 + [(lon, BF16)] * 2
    start = (lax.axis_index("month") * levels).astype(jnp.int32)[None]
    vmem, smem = pl.BlockSpec(memory_space=pltpu.VMEM), pl.BlockSpec(memory_space=pltpu.SMEM)
    field_a, field_b, field_s, wet, rate, *sent = call(
        functools.partial(init_body, levels, columns),
        [(inner, F32), (outer, F32), (sides, F32), ((levels, columns, lat), F32), (row, F32)] + messages,
        2 * 10**6,
        in_specs=[smem] * 2 + [vmem] * 3 + [pl.BlockSpec(memory_space=pl.ANY)],
        scratch=[pltpu.VMEM(state.shape, F32), pltpu.SemaphoreType.DMA],
    )(start, rates, land_mask, wet_levels, state, basis)
    (gram,) = call(gram_body, [((1, 128), F32)], 2 * 10**6)(basis_rows)
    parts[0] = after(parts[0], gram)
    place = lax.axis_index("tracer").astype(jnp.int32)[None]

    def fetched(part):
        return [part] + [shifted(part, "tracer", k, True) for k in range(1, n_tracer)]

    def prepared(pieces):
        return call(
            lambda *refs: prepare_body(refs[:-1], refs[-1]),
            [((27, levels, columns, lat), F32)],
            2 * 10**6,
            in_specs=[smem] + [vmem] * n_tracer,
        )(place, *pieces)[0]

    inner_levels, outer_levels = list(range(1, levels - 1)), [0, levels - 1]
    steps = coefficients.shape[0] * n_month
    pieces = [fetched(parts[0])]
    for month in range(1, steps):
        pieces.append(fetched(after(parts[month], *pieces[-1])))
    for month in range(steps):
        weights = prepared(pieces[month])
        lev_lo, lev_hi, lon_lo, lon_hi = sent
        below, above = shifted(lev_hi, "month", 1), shifted(lev_lo, "month", -1)
        args = (weights, field_a, field_b, field_s, rate, wet)

        def part(mine, shape, is_outer, *more):
            return call(
                functools.partial(part_body, levels, columns, mine, is_outer), [(shape, F32)], 10**7
            )(*args, *more)[0]

        new_a = part(inner_levels, inner, False)
        left, right = call(
            functools.partial(pack_body, columns),
            [((2, levels + 2) + row, BF16)] * 2,
            10**5,
            in_specs=[pl.BlockSpec(memory_space=pl.ANY)] + [vmem] * 4,
        )(new_a if month else wet, below, above, lon_lo, lon_hi)
        left, right = shifted(right, "space", 1), shifted(left, "space", -1)
        new_b = part(outer_levels, outer, True, below, above)
        field_a, field_b = new_a, new_b
        ends = (new_a, new_b, weights, left, right, wet)
        if month < steps - 1:
            field_s, *sent = call(
                functools.partial(side_body, levels, columns), [(sides, F32)] + messages, 2 * 10**6
            )(*ends)

    residual, product, tiles = call(
        functools.partial(last_body, levels, columns),
        [(state.shape, F32)] * 2 + [((n_month, 1, 128), F32)],
        4 * 10**6,
        scratch=[pltpu.VMEM(state.shape, F32)] * 2,
    )(*ends, state, basis, gram)

    def total(tiles):
        part = jnp.sum(spread(tiles, "month"), axis=0)
        return spread(copies(part, n_space * n_tracer), ("space", "tracer"))

    cells = float(state.size * n_space * n_tracer * n_month)
    remainder, next_basis, krylov, sure = call(
        functools.partial(finish_body, cells), [(flat, F32)] * 2 + [((1, count + 2), F32), ((1, 1), F32)], 2 * 10**6
    )(total(tiles), product.reshape(flat), basis_rows)

    def direct(remainder, next_basis, krylov):
        own = jnp.broadcast_to(jnp.sum(remainder * remainder), (n_month, 1, 128))
        norm = jnp.sqrt(jnp.sum(total(own), axis=0)[0, 0] / cells + 1e-06)
        return remainder / norm, jnp.where(jnp.arange(count + 2) == count, norm, krylov)

    next_basis, krylov = lax.cond(
        sure[0, 0] > 0.5, lambda r, n, k: (n, k), direct, remainder, next_basis, krylov
    )
    return residual, next_basis.reshape(state.shape), krylov.reshape(count + 2)


def solution(mesh):
    return jax.shard_map(
        on_device,
        mesh=mesh,
        in_specs=(
            P("tracer", "month", "space", None),
            P("month", None, None, "space", None),
            P("tracer"),
            P("space", None),
            P("space", None),
            P(None, "tracer", "month", "space", None),
        ),
        out_specs=(P("tracer", "month", "space", None), P("tracer", "month", "space", None), P()),
        check_vma=False,
    )
```

```python
import functools

import jax
import jax.numpy as jnp
from jax import lax
from jax.experimental import pallas as pl
from jax.experimental.pallas import tpu as pltpu
from jax.sharding import PartitionSpec as P

F32 = jnp.float32
BF16 = jnp.bfloat16
TAPS = [(dl, di) for dl in (-1, 0, 1) for di in (-1, 0, 1)]


VMEM_LIMIT = 20 * 2**20


def call(body, outs, cost, scratch=(), in_specs=None):
    return pl.pallas_call(
        body,
        out_shape=[jax.ShapeDtypeStruct(s, d) for s, d in outs],
        scratch_shapes=list(scratch),
        cost_estimate=pl.CostEstimate(flops=cost, transcendentals=0, bytes_accessed=cost // 8),
        compiler_params=pltpu.CompilerParams(vmem_limit_bytes=VMEM_LIMIT),
        **({} if in_specs is None else {"in_specs": in_specs}),
    )


def keep_of(axis):
    place = lax.axis_index(axis)
    return [jnp.where(place > 0, 1.0, 0.0), jnp.where(place < lax.axis_size(axis) - 1, 1.0, 0.0)]


def reader(levels, columns, inner_ref, outer_ref, sides_ref):
    def get(f, l, i):
        if i in (0, columns - 1):
            return sides_ref[f, l, int(i > 0)]
        if l in (0, levels - 1):
            return outer_ref[f, int(l > 0), i]
        return inner_ref[f, l - 1, i]

    return get


def init_body(levels, columns, rates_ref, land_ref, depth_ref, state_ref, basis_ref, *outs):
    inner_ref, outer_ref, sides_ref, wet_ref, rate_ref, lev_lo, lev_hi, lon_lo, lon_hi, last_ref, sem = outs
    fetch = pltpu.make_async_copy(basis_ref.at[basis_ref.shape[0] - 1], last_ref, sem)
    fetch.start()
    tracer = lax.broadcasted_iota(jnp.int32, rate_ref.shape, 0)
    rate = jnp.zeros(rate_ref.shape, F32)
    for n in range(rate_ref.shape[0]):
        rate = jnp.where(tracer == n, rates_ref[n], rate)
    rate_ref[...] = rate
    for l in range(levels):
        ocean = (land_ref[...] == 1) & (lax.axis_index("month") * levels + l < depth_ref[...])
        wet_ref[l] = jnp.where(ocean, 1.0, 0.0).astype(F32)
    for f, ref in enumerate((state_ref, last_ref)):
        if f:
            fetch.wait()
        for l in range(levels):
            rows = pltpu.einshape("tix->itx", ref[:, l])
            for i in range(columns):
                row = rows[i] * wet_ref[l, pl.ds(i, 1), :]
                short = row.astype(BF16)
                if i in (0, columns - 1):
                    sides_ref[f, l, int(i > 0)] = row
                    (lon_hi if i else lon_lo)[f, l] = short
                elif l in (0, levels - 1):
                    outer_ref[f, int(l > 0), i] = row
                else:
                    inner_ref[f, l - 1, i] = row
                if l in (0, levels - 1):
                    (lev_hi if l else lev_lo)[f, i] = short


def combine(sums):
    n = sums[1].shape[1]
    return sums[1] + pltpu.roll(sums[2], n - 1, 1) + pltpu.roll(sums[0], 1, 1)


def tap_sums(taps):
    acc = [[None] * 3, [None] * 3]
    for weights, rows in taps:
        for dj in range(3):
            for f in range(2):
                term = weights[dj] * rows[f]
                acc[f][dj] = term if acc[f][dj] is None else acc[f][dj] + term
    return combine(acc[0]), combine(acc[1])


def prepare_body(w_refs, wf_ref):
    parts = w_refs
    size = parts[0].shape[3]
    taps, levels, columns, lat = wf_ref.shape
    for n, ref in enumerate(parts):
        place = lax.rem(lax.axis_index("tracer") - n + len(parts), len(parts))
        lanes = pl.ds(pl.multiple_of(place * size, size), size)

        def spread_part(k, carry, ref=ref, lanes=lanes):
            for l in range(levels):
                wf_ref[k, l, :, lanes] = ref[k, l].astype(F32)
            return carry

        lax.fori_loop(0, taps, spread_part, 0, unroll=3)
    lane = lax.broadcasted_iota(jnp.int32, (columns, lat), 1)

    def move(k, carry):
        for l in range(levels):
            wf_ref[3 * k + 2, l] = jnp.where(lane == 0, 0.0, pltpu.roll(wf_ref[3 * k + 2, l], 1, 1))
            wf_ref[3 * k, l] = jnp.where(lane == lat - 1, 0.0, pltpu.roll(wf_ref[3 * k, l], lat - 1, 1))
        return carry

    lax.fori_loop(0, taps // 3, move, 0, unroll=3)


def part_body(levels, columns, mine, outer, wf_ref, inner_ref, outer_ref, sides_ref, rate_ref, wet_ref, *rest):
    if outer:
        below_ref, above_ref, out_ref = rest
    else:
        (out_ref,) = rest
    get = reader(levels, columns, inner_ref, outer_ref, sides_ref)
    keep = keep_of("month")
    rate = rate_ref[...]

    def rows_at(l, i):
        if l < 0:
            return [below_ref[f, i].astype(F32) * keep[0] for f in range(2)]
        if l >= levels:
            return [above_ref[f, i].astype(F32) * keep[1] for f in range(2)]
        return [get(f, l, i) for f in range(2)]

    for n, l in enumerate(mine):
        for i in range(columns):
            taps = []
            for dl, di in TAPS:
                if 0 <= i + di < columns:
                    first = 9 * (dl + 1) + 3 * (di + 1)
                    weights = [wf_ref[first + dj, l, pl.ds(i, 1), :] for dj in range(3)]
                    taps.append((weights, rows_at(l + dl, i + di)))
            ac, at = tap_sums(taps)
            c, t = rows_at(l, i)
            square = c * c
            inverse = 1.0 / (1.0 + square)
            part = rate * square * inverse
            ac = ac - part * c
            at = at - part * inverse * (3.0 + square) * t
            if 0 < i < columns - 1:
                wet = wet_ref[l, pl.ds(i, 1), :]
                ac, at = ac * wet, at * wet
            out_ref[0, n, i] = ac
            out_ref[1, n, i] = at


def side_rows(levels, columns, inner_ref, outer_ref, wf_ref, left_ref, right_ref, wet_ref):
    keep_lev, keep_lon = keep_of("month"), keep_of("space")
    for l in range(levels):
        edge = l in (0, levels - 1)
        n = int(l > 0) if edge else l - 1
        own = outer_ref if edge else inner_ref
        for side, i in ((0, 0), (1, columns - 1)):
            halo = (left_ref, right_ref)[side]
            taps = []
            for d in range(3):
                keep = keep_lon[side]
                if not 0 <= l + d - 1 < levels:
                    keep = keep * keep_lev[int(l + d > levels)]
                weights = [wf_ref[9 * d + 6 * side + dj, l, pl.ds(i, 1), :] for dj in range(3)]
                taps.append((weights, [halo[f, l + d].astype(F32) * keep for f in range(2)]))
            sums = tap_sums(taps)
            wet = wet_ref[l, pl.ds(i, 1), :]
            yield l, side, i, [(own[f, n, i] + sums[f]) * wet for f in range(2)]


def side_body(levels, columns, *refs):
    sides_ref, lev_lo, lev_hi, lon_lo, lon_hi = refs[6:]
    outer_ref = refs[1]
    for l, side, i, rows in side_rows(levels, columns, *refs[:6]):
        for f in range(2):
            short = rows[f].astype(BF16)
            sides_ref[f, l, side] = rows[f]
            (lon_hi if side else lon_lo)[f, l] = short
            if l in (0, levels - 1):
                (lev_hi if l else lev_lo)[f, i] = short
    for f in range(2):
        for i in range(1, columns - 1):
            lev_lo[f, i] = outer_ref[f, 0, i].astype(BF16)
            lev_hi[f, i] = outer_ref[f, 1, i].astype(BF16)


def pack_body(columns, after_ref, below_ref, above_ref, lo_ref, hi_ref, left_out, right_out):
    levels = lo_ref.shape[1]
    for out, own, i in ((left_out, lo_ref, 0), (right_out, hi_ref, columns - 1)):
        for f in range(2):
            out[f, 0] = below_ref[f, i]
            out[f, levels + 1] = above_ref[f, i]
            for l in range(levels):
                out[f, l + 1] = own[f, l]


def lanes_of(values, first):
    lane = lax.broadcasted_iota(jnp.int32, (1, 128), 1)
    total = jnp.zeros((1, 128), F32)
    for n, v in enumerate(values):
        total = jnp.where(lane == first + n, v, total)
    return total


def gram_body(basis_ref, out_ref):
    count = basis_ref.shape[0]
    pairs = [(k, m) for k in range(count) for m in range(k, count)]

    def step(n, acc):
        rows = pl.ds(pl.multiple_of(n * 8, 8), 8)
        b = [basis_ref[k, rows, :] for k in range(count)]
        return tuple(a + b[k] * b[m] for a, (k, m) in zip(acc, pairs))

    zero = jnp.zeros((8, basis_ref.shape[2]), F32)
    acc = lax.fori_loop(0, basis_ref.shape[1] // 8, step, (zero,) * len(pairs))
    out_ref[...] = lanes_of([jnp.sum(a) for a in acc], 6)


def last_body(levels, columns, *refs):
    state_ref, basis_ref, gram_ref, res_ref, prod_ref, out_ref = refs[6:12]
    fields = refs[12:]
    inner_ref, outer_ref = refs[:2]
    sides = {}
    for l, side, i, rows in side_rows(levels, columns, *refs[:6]):
        sides[l, i] = rows
    for l in range(levels):
        for f in range(2):
            own = [sides[l, i][f] if i in (0, columns - 1)
                   else outer_ref[f, int(l > 0), i] if l in (0, levels - 1) else inner_ref[f, l - 1, i]
                   for i in range(columns)]
            fields[f][:, l] = pltpu.einshape("itx->tix", jnp.stack(own))
    count = basis_ref.shape[0]

    def step(n, acc):
        for l in range(levels):
            b = [basis_ref[k, n, l] for k in range(count)]
            residual = fields[0][n, l] - state_ref[n, l]
            product = fields[1][n, l] - b[count - 1]
            res_ref[n, l] = residual
            prod_ref[n, l] = product
            terms = [x * product for x in b] + [product * product, residual * residual]
            acc = tuple(a + x for a, x in zip(acc, terms))
        return acc

    zero = jnp.zeros(fields[0].shape[2:], F32)
    acc = lax.fori_loop(0, fields[0].shape[0], step, (zero,) * (count + 2))
    row = gram_ref[...] + lanes_of([jnp.sum(a) for a in acc], 0)
    for n in range(out_ref.shape[0]):
        out_ref[n] = row


def finish_body(cells, rows_ref, prod_ref, basis_ref, rem_ref, next_ref, krylov_ref, sure_ref):
    count = basis_ref.shape[0]
    means = rows_ref[0]
    for n in range(1, rows_ref.shape[0]):
        means = means + rows_ref[n]
    means = means / cells
    lane = lax.broadcasted_iota(jnp.int32, (1, 128), 1)

    def pick(n):
        return jnp.sum(jnp.where(lane == n, means, 0.0), axis=1, keepdims=True)

    coef = [pick(k) for k in range(count)]
    cross = sum(2.0 * c * c for c in coef)
    gram = 0.0
    place = count + 2
    for k in range(count):
        for m in range(k, count):
            gram = gram + (1.0 if k == m else 2.0) * coef[k] * coef[m] * pick(place)
            place += 1
    square = pick(count)
    expanded = square - cross + gram
    sure = jnp.where(expanded > 0.01 * (square + cross + gram), 1.0, 0.0)
    norm = jnp.sqrt(jnp.maximum(expanded, 0.0) + 1e-06)
    rms = jnp.sqrt(pick(count + 1) + 1e-06)
    krylov = jnp.where(lane == count, norm, jnp.where(lane == count + 1, rms, means))
    krylov_ref[...] = krylov[:, : count + 2]
    sure_ref[...] = sure
    inverse = 1.0 / norm

    def step(n, carry):
        rows = pl.ds(pl.multiple_of(n * 8, 8), 8)
        rem = coef[0] * basis_ref[0, rows, :]
        for k in range(1, count):
            rem = rem + coef[k] * basis_ref[k, rows, :]
        rem = prod_ref[rows, :] - rem
        rem_ref[rows, :] = rem
        next_ref[rows, :] = rem * inverse
        return carry

    lax.fori_loop(0, prod_ref.shape[0] // 8, step, 0)


def spread(x, axes):
    return lax.all_to_all(x, axes, 0, 0, tiled=True)


def copies(x, count):
    return jnp.broadcast_to(x[None], (count,) + x.shape)


def shifted(x, axis, by):
    size = lax.axis_size(axis)
    return lax.ppermute(x, axis, [(n, (n + by) % size) for n in range(size)])


def after(x, *others):
    return lax.optimization_barrier((x, *others))[0]


def extract_body(coef_ref, *refs):
    outs, sem = refs[:-1], refs[-1]
    levels, part = outs[0].shape[1], outs[0].shape[3]
    place = pl.ds(pl.multiple_of(lax.axis_index("tracer") * part, part), part)
    fetches = []
    for k, out in enumerate(outs):
        level = pl.ds(lax.rem(lax.axis_index("month") + k, len(outs)) * levels, levels)
        fetches.append(pltpu.make_async_copy(coef_ref.at[0, :, level, :, place], out, sem.at[k]))
        fetches[-1].start()
    for fetch in fetches:
        fetch.wait()


def month_parts(coefficients, levels):
    taps, all_levels, columns, lat = coefficients.shape[1:]
    n_tracer, n_month = lax.axis_size("tracer"), lax.axis_size("month")
    own = call(
        extract_body,
        [((taps, levels, columns, lat // n_tracer), BF16)] * n_month,
        10**6,
        scratch=[pltpu.SemaphoreType.DMA((n_month,))],
        in_specs=[pl.BlockSpec(memory_space=pl.ANY)],
    )(coefficients)
    return [own[0]] + [shifted(own[k], "month", k) for k in range(1, n_month)]


def select_body(month, *refs):
    found, out = refs[:-1], refs[-1]
    place = lax.rem(lax.axis_index("month") - month + len(found), len(found))
    for k, ref in enumerate(found):

        @pl.when(place == k)
        def _(ref=ref):
            out[...] = ref[...]


def of_month(found, month):
    return call(functools.partial(select_body, month), [(found[0].shape, BF16)], 10**5)(*found)[0]


def on_device(state, coefficients, rates, land_mask, wet_levels, basis):
    tracers, levels, columns, lat = state.shape
    count = basis.shape[0]
    n_space, n_month, n_tracer = lax.axis_size("space"), lax.axis_size("month"), lax.axis_size("tracer")
    flat = (tracers * levels * columns, lat)
    basis_rows = basis.reshape((count,) + flat)
    found = month_parts(coefficients, levels)

    row = (tracers, lat)
    inner, outer = (2, levels - 2, columns) + row, (2, 2, columns) + row
    sides, lev, lon = (2, levels, 2) + row, (2, columns) + row, (2, levels) + row
    messages = [(lev, BF16)] * 2 + [(lon, BF16)] * 2
    vmem, smem = pl.BlockSpec(memory_space=pltpu.VMEM), pl.BlockSpec(memory_space=pltpu.SMEM)
    anywhere = pl.BlockSpec(memory_space=pl.ANY)
    field_a, field_b, field_s, wet, rate, *sent = call(
        functools.partial(init_body, levels, columns),
        [(inner, F32), (outer, F32), (sides, F32), ((levels, columns, lat), F32), (row, F32)] + messages,
        2 * 10**6,
        in_specs=[smem] + [vmem] * 3 + [anywhere],
        scratch=[pltpu.VMEM(state.shape, F32), pltpu.SemaphoreType.DMA],
    )(rates, land_mask, wet_levels, state, basis)
    (gram,) = call(gram_body, [((1, 128), F32)], 2 * 10**6)(basis_rows)
    def fetched(part):
        return [part] + [shifted(part, "tracer", k) for k in range(1, n_tracer)]

    def prepared(pieces):
        return call(
            lambda *refs: prepare_body(refs[:-1], refs[-1]),
            [((27, levels, columns, lat), F32)],
            2 * 10**6,
        )(*pieces)[0]

    inner_levels, outer_levels = list(range(1, levels - 1)), [0, levels - 1]
    steps = coefficients.shape[0] * n_month
    halos = shifted(sent[1], "month", 1), shifted(sent[0], "month", -1)
    pieces = [fetched(after(of_month(found, 0), gram, *halos))]
    for month in range(1, steps):
        found = lax.optimization_barrier((found, pieces[-1]))[0]
        pieces.append(fetched(of_month(found, month)))
    for month in range(steps):
        weights = prepared(pieces[month])
        lev_lo, lev_hi, lon_lo, lon_hi = sent
        below, above = halos if month == 0 else (shifted(lev_hi, "month", 1), shifted(lev_lo, "month", -1))
        args = (weights, field_a, field_b, field_s, rate, wet)

        def part(mine, shape, is_outer, *more):
            return call(
                functools.partial(part_body, levels, columns, mine, is_outer),
                [(shape, F32)],
                10**7,
            )(*args, *more)[0]

        new_a = part(inner_levels, inner, False)
        left, right = call(
            functools.partial(pack_body, columns),
            [((2, levels + 2) + row, BF16)] * 2,
            10**5,
            in_specs=[anywhere] + [vmem] * 4,
        )(new_a if month else wet, below, above, lon_lo, lon_hi)
        left, right = shifted(right, "space", 1), shifted(left, "space", -1)
        new_b = part(outer_levels, outer, True, below, above)
        field_a, field_b = new_a, new_b
        ends = (new_a, new_b, weights, left, right, wet)
        if month < steps - 1:
            field_s, *sent = call(
                functools.partial(side_body, levels, columns), [(sides, F32)] + messages, 2 * 10**6,
            )(*ends)

    residual, product, tiles = call(
        functools.partial(last_body, levels, columns),
        [(state.shape, F32)] * 2 + [((n_month, 1, 128), F32)],
        4 * 10**6,
        scratch=[pltpu.VMEM(state.shape, F32)] * 2,
    )(*ends, state, basis, gram)

    def total(tiles):
        part = jnp.sum(spread(tiles, "month"), axis=0)
        return spread(copies(part, n_space * n_tracer), ("space", "tracer"))

    cells = float(state.size * n_space * n_tracer * n_month)
    remainder, next_basis, krylov, sure = call(
        functools.partial(finish_body, cells), [(flat, F32)] * 2 + [((1, count + 2), F32), ((1, 1), F32)], 2 * 10**6
    )(total(tiles), product.reshape(flat), basis_rows)

    def direct(remainder, next_basis, krylov):
        own = jnp.broadcast_to(jnp.sum(remainder * remainder), (n_month, 1, 128))
        norm = jnp.sqrt(jnp.sum(total(own), axis=0)[0, 0] / cells + 1e-06)
        return remainder / norm, jnp.where(jnp.arange(count + 2) == count, norm, krylov)

    next_basis, krylov = lax.cond(
        sure[0, 0] > 0.5, lambda r, n, k: (n, k), direct, remainder, next_basis, krylov
    )
    return residual, next_basis.reshape(state.shape), krylov.reshape(count + 2)


def solution(mesh):
    return jax.shard_map(
        on_device,
        mesh=mesh,
        in_specs=(
            P("tracer", "month", "space", None),
            P("month", None, None, "space", None),
            P("tracer"),
            P("space", None),
            P("space", None),
            P(None, "tracer", "month", "space", None),
        ),
        out_specs=(P("tracer", "month", "space", None), P("tracer", "month", "space", None), P()),
        check_vma=False,
    )
```

```python
import functools

import jax
import jax.numpy as jnp
from jax import lax
from jax.experimental import pallas as pl
from jax.experimental.pallas import tpu as pltpu
from jax.sharding import PartitionSpec as P

F32 = jnp.float32
BF16 = jnp.bfloat16
TAPS = [(dl, di) for dl in (-1, 0, 1) for di in (-1, 0, 1)]


VMEM_LIMIT = 20 * 2**20


def call(body, outs, cost, scratch=(), in_specs=None):
    return pl.pallas_call(
        body,
        out_shape=[jax.ShapeDtypeStruct(s, d) for s, d in outs],
        scratch_shapes=list(scratch),
        cost_estimate=pl.CostEstimate(flops=cost, transcendentals=0, bytes_accessed=cost // 8),
        compiler_params=pltpu.CompilerParams(vmem_limit_bytes=VMEM_LIMIT),
        **({} if in_specs is None else {"in_specs": in_specs}),
    )


def keep_of(axis):
    place = lax.axis_index(axis)
    return [jnp.where(place > 0, 1.0, 0.0), jnp.where(place < lax.axis_size(axis) - 1, 1.0, 0.0)]


def reader(levels, columns, inner_ref, outer_ref, sides_ref):
    def get(f, l, i):
        if i in (0, columns - 1):
            return sides_ref[f, l, int(i > 0)]
        if l in (0, levels - 1):
            return outer_ref[f, int(l > 0), i]
        return inner_ref[f, l - 1, i]

    return get


def init_body(levels, columns, rates_ref, land_ref, depth_ref, state_ref, basis_ref, *outs):
    inner_ref, outer_ref, sides_ref, wet_ref, rate_ref, lev_lo, lev_hi, lon_lo, lon_hi, last_ref, sem = outs
    fetch = pltpu.make_async_copy(basis_ref.at[basis_ref.shape[0] - 1], last_ref, sem)
    fetch.start()
    tracer = lax.broadcasted_iota(jnp.int32, rate_ref.shape, 0)
    rate = jnp.zeros(rate_ref.shape, F32)
    for n in range(rate_ref.shape[0]):
        rate = jnp.where(tracer == n, rates_ref[n], rate)
    rate_ref[...] = rate
    for l in range(levels):
        ocean = (land_ref[...] == 1) & (lax.axis_index("month") * levels + l < depth_ref[...])
        wet_ref[l] = jnp.where(ocean, 1.0, 0.0).astype(F32)
    for f, ref in enumerate((state_ref, last_ref)):
        if f:
            fetch.wait()
        for l in range(levels):
            rows = pltpu.einshape("tix->itx", ref[:, l])
            for i in range(columns):
                row = rows[i] * wet_ref[l, pl.ds(i, 1), :]
                short = row.astype(BF16)
                if i in (0, columns - 1):
                    sides_ref[f, l, int(i > 0)] = row
                    (lon_hi if i else lon_lo)[f, l] = short
                elif l in (0, levels - 1):
                    outer_ref[f, int(l > 0), i] = row
                else:
                    inner_ref[f, l - 1, i] = row
                if l in (0, levels - 1):
                    (lev_hi if l else lev_lo)[f, i] = short


def combine(sums):
    n = sums[1].shape[1]
    return sums[1] + pltpu.roll(sums[2], n - 1, 1) + pltpu.roll(sums[0], 1, 1)


def tap_sums(taps):
    acc = [[None] * 3, [None] * 3]
    for weights, rows in taps:
        for dj in range(3):
            for f in range(2):
                term = weights[dj] * rows[f]
                acc[f][dj] = term if acc[f][dj] is None else acc[f][dj] + term
    return combine(acc[0]), combine(acc[1])


def prepare_body(w_refs, wf_ref, n_in):
    parts = w_refs
    size = parts[0].shape[4]
    taps, levels, columns, lat = wf_ref.shape
    for n, ref in enumerate(parts):
        place = lax.rem(lax.axis_index("tracer") - n + len(parts), len(parts))
        lanes = pl.ds(pl.multiple_of(place * size, size), size)

        def spread_part(k, carry, ref=ref, lanes=lanes):
            for l in range(levels):
                wf_ref[k, l, :, lanes] = ref[n_in, k, l].astype(F32)
            return carry

        lax.fori_loop(0, taps, spread_part, 0, unroll=3)
    lane = lax.broadcasted_iota(jnp.int32, (columns, lat), 1)

    def move(k, carry):
        for l in range(levels):
            wf_ref[3 * k + 2, l] = jnp.where(lane == 0, 0.0, pltpu.roll(wf_ref[3 * k + 2, l], 1, 1))
            wf_ref[3 * k, l] = jnp.where(lane == lat - 1, 0.0, pltpu.roll(wf_ref[3 * k, l], lat - 1, 1))
        return carry

    lax.fori_loop(0, taps // 3, move, 0, unroll=3)


def part_body(levels, columns, mine, outer, wf_ref, inner_ref, outer_ref, sides_ref, rate_ref, wet_ref, *rest):
    if outer:
        below_ref, above_ref, out_ref = rest
    else:
        (out_ref,) = rest
    get = reader(levels, columns, inner_ref, outer_ref, sides_ref)
    keep = keep_of("month")
    rate = rate_ref[...]

    def rows_at(l, i):
        if l < 0:
            return [below_ref[f, i].astype(F32) * keep[0] for f in range(2)]
        if l >= levels:
            return [above_ref[f, i].astype(F32) * keep[1] for f in range(2)]
        return [get(f, l, i) for f in range(2)]

    for n, l in enumerate(mine):
        for i in range(columns):
            taps = []
            for dl, di in TAPS:
                if 0 <= i + di < columns:
                    first = 9 * (dl + 1) + 3 * (di + 1)
                    weights = [wf_ref[first + dj, l, pl.ds(i, 1), :] for dj in range(3)]
                    taps.append((weights, rows_at(l + dl, i + di)))
            ac, at = tap_sums(taps)
            c, t = rows_at(l, i)
            square = c * c
            inverse = 1.0 / (1.0 + square)
            part = rate * square * inverse
            ac = ac - part * c
            at = at - part * inverse * (3.0 + square) * t
            if 0 < i < columns - 1:
                wet = wet_ref[l, pl.ds(i, 1), :]
                ac, at = ac * wet, at * wet
            out_ref[0, n, i] = ac
            out_ref[1, n, i] = at


def side_rows(levels, columns, inner_ref, outer_ref, wf_ref, left_ref, right_ref, wet_ref):
    keep_lev, keep_lon = keep_of("month"), keep_of("space")
    for l in range(levels):
        edge = l in (0, levels - 1)
        n = int(l > 0) if edge else l - 1
        own = outer_ref if edge else inner_ref
        for side, i in ((0, 0), (1, columns - 1)):
            halo = (left_ref, right_ref)[side]
            taps = []
            for d in range(3):
                keep = keep_lon[side]
                if not 0 <= l + d - 1 < levels:
                    keep = keep * keep_lev[int(l + d > levels)]
                weights = [wf_ref[9 * d + 6 * side + dj, l, pl.ds(i, 1), :] for dj in range(3)]
                taps.append((weights, [halo[f, l + d].astype(F32) * keep for f in range(2)]))
            sums = tap_sums(taps)
            wet = wet_ref[l, pl.ds(i, 1), :]
            yield l, side, i, [(own[f, n, i] + sums[f]) * wet for f in range(2)]


def side_body(levels, columns, *refs):
    sides_ref, lev_lo, lev_hi, lon_lo, lon_hi = refs[6:]
    outer_ref = refs[1]
    for l, side, i, rows in side_rows(levels, columns, *refs[:6]):
        for f in range(2):
            short = rows[f].astype(BF16)
            sides_ref[f, l, side] = rows[f]
            (lon_hi if side else lon_lo)[f, l] = short
            if l in (0, levels - 1):
                (lev_hi if l else lev_lo)[f, i] = short
    for f in range(2):
        for i in range(1, columns - 1):
            lev_lo[f, i] = outer_ref[f, 0, i].astype(BF16)
            lev_hi[f, i] = outer_ref[f, 1, i].astype(BF16)


def pack_body(columns, after_ref, below_ref, above_ref, lo_ref, hi_ref, left_out, right_out):
    levels = lo_ref.shape[1]
    for out, own, i in ((left_out, lo_ref, 0), (right_out, hi_ref, columns - 1)):
        for f in range(2):
            out[f, 0] = below_ref[f, i]
            out[f, levels + 1] = above_ref[f, i]
            for l in range(levels):
                out[f, l + 1] = own[f, l]


def lanes_of(values, first):
    lane = lax.broadcasted_iota(jnp.int32, (1, 128), 1)
    total = jnp.zeros((1, 128), F32)
    for n, v in enumerate(values):
        total = jnp.where(lane == first + n, v, total)
    return total


def gram_body(basis_ref, out_ref):
    count = basis_ref.shape[0]
    pairs = [(k, m) for k in range(count) for m in range(k, count)]

    def step(n, acc):
        rows = pl.ds(pl.multiple_of(n * 8, 8), 8)
        b = [basis_ref[k, rows, :] for k in range(count)]
        return tuple(a + b[k] * b[m] for a, (k, m) in zip(acc, pairs))

    zero = jnp.zeros((8, basis_ref.shape[2]), F32)
    acc = lax.fori_loop(0, basis_ref.shape[1] // 8, step, (zero,) * len(pairs))
    out_ref[...] = lanes_of([jnp.sum(a) for a in acc], 6)


def last_body(levels, columns, *refs):
    state_ref, basis_ref, gram_ref, res_ref, prod_ref, out_ref = refs[6:12]
    fields = refs[12:]
    inner_ref, outer_ref = refs[:2]
    sides = {}
    for l, side, i, rows in side_rows(levels, columns, *refs[:6]):
        sides[l, i] = rows
    for l in range(levels):
        for f in range(2):
            own = [sides[l, i][f] if i in (0, columns - 1)
                   else outer_ref[f, int(l > 0), i] if l in (0, levels - 1) else inner_ref[f, l - 1, i]
                   for i in range(columns)]
            fields[f][:, l] = pltpu.einshape("itx->tix", jnp.stack(own))
    count = basis_ref.shape[0]

    def step(n, acc):
        for l in range(levels):
            b = [basis_ref[k, n, l] for k in range(count)]
            residual = fields[0][n, l] - state_ref[n, l]
            product = fields[1][n, l] - b[count - 1]
            res_ref[n, l] = residual
            prod_ref[n, l] = product
            terms = [x * product for x in b] + [product * product, residual * residual]
            acc = tuple(a + x for a, x in zip(acc, terms))
        return acc

    zero = jnp.zeros(fields[0].shape[2:], F32)
    acc = lax.fori_loop(0, fields[0].shape[0], step, (zero,) * (count + 2))
    row = gram_ref[...] + lanes_of([jnp.sum(a) for a in acc], 0)
    for n in range(out_ref.shape[0]):
        out_ref[n] = row


def finish_body(cells, rows_ref, prod_ref, basis_ref, rem_ref, next_ref, krylov_ref, sure_ref):
    count = basis_ref.shape[0]
    means = rows_ref[0]
    for n in range(1, rows_ref.shape[0]):
        means = means + rows_ref[n]
    means = means / cells
    lane = lax.broadcasted_iota(jnp.int32, (1, 128), 1)

    def pick(n):
        return jnp.sum(jnp.where(lane == n, means, 0.0), axis=1, keepdims=True)

    coef = [pick(k) for k in range(count)]
    cross = sum(2.0 * c * c for c in coef)
    gram = 0.0
    place = count + 2
    for k in range(count):
        for m in range(k, count):
            gram = gram + (1.0 if k == m else 2.0) * coef[k] * coef[m] * pick(place)
            place += 1
    square = pick(count)
    expanded = square - cross + gram
    sure = jnp.where(expanded > 0.01 * (square + cross + gram), 1.0, 0.0)
    norm = jnp.sqrt(jnp.maximum(expanded, 0.0) + 1e-06)
    rms = jnp.sqrt(pick(count + 1) + 1e-06)
    krylov = jnp.where(lane == count, norm, jnp.where(lane == count + 1, rms, means))
    krylov_ref[...] = krylov[:, : count + 2]
    sure_ref[...] = sure
    inverse = 1.0 / norm

    def step(n, carry):
        rows = pl.ds(pl.multiple_of(n * 8, 8), 8)
        rem = coef[0] * basis_ref[0, rows, :]
        for k in range(1, count):
            rem = rem + coef[k] * basis_ref[k, rows, :]
        rem = prod_ref[rows, :] - rem
        rem_ref[rows, :] = rem
        next_ref[rows, :] = rem * inverse
        return carry

    lax.fori_loop(0, prod_ref.shape[0] // 8, step, 0)


def spread(x, axes):
    return lax.all_to_all(x, axes, 0, 0, tiled=True)


def copies(x, count):
    return jnp.broadcast_to(x[None], (count,) + x.shape)


def shifted(x, axis, by):
    size = lax.axis_size(axis)
    return lax.ppermute(x, axis, [(n, (n + by) % size) for n in range(size)])


def after(x, *others):
    return lax.optimization_barrier((x, *others))[0]


def extract_body(coef_ref, *refs):
    outs, sem = refs[:-1], refs[-1]
    levels, part = outs[0].shape[1], outs[0].shape[3]
    place = pl.ds(pl.multiple_of(lax.axis_index("tracer") * part, part), part)
    fetches = []
    for k, out in enumerate(outs):
        level = pl.ds(lax.rem(lax.axis_index("month") + k, len(outs)) * levels, levels)
        fetches.append(pltpu.make_async_copy(coef_ref.at[0, :, level, :, place], out, sem.at[k]))
        fetches[-1].start()
    for fetch in fetches:
        fetch.wait()


def month_parts(coefficients, levels):
    taps, all_levels, columns, lat = coefficients.shape[1:]
    n_tracer, n_month = lax.axis_size("tracer"), lax.axis_size("month")
    own = call(
        extract_body,
        [((taps, levels, columns, lat // n_tracer), BF16)] * n_month,
        10**6,
        scratch=[pltpu.SemaphoreType.DMA((n_month,))],
        in_specs=[pl.BlockSpec(memory_space=pltpu.HBM)],
    )(coefficients)
    return [own[0]] + [shifted(own[k], "month", k) for k in range(1, n_month)]


def select_body(months, *refs):
    found, out = refs[:-1], refs[-1]
    for n, month in enumerate(months):
        place = lax.rem(lax.axis_index("month") - month + len(found), len(found))
        for k, ref in enumerate(found):

            @pl.when(place == k)
            def _(ref=ref, n=n):
                out[n] = ref[...]


def of_months(found, months):
    shape = (len(months),) + found[0].shape
    return call(functools.partial(select_body, months), [(shape, BF16)], 10**5)(*found)[0]


def on_device(state, coefficients, rates, land_mask, wet_levels, basis):
    tracers, levels, columns, lat = state.shape
    count = basis.shape[0]
    n_space, n_month, n_tracer = lax.axis_size("space"), lax.axis_size("month"), lax.axis_size("tracer")
    flat = (tracers * levels * columns, lat)
    basis_rows = basis.reshape((count,) + flat)
    found = month_parts(coefficients, levels)

    row = (tracers, lat)
    inner, outer = (2, levels - 2, columns) + row, (2, 2, columns) + row
    sides, lev, lon = (2, levels, 2) + row, (2, columns) + row, (2, levels) + row
    messages = [(lev, BF16)] * 2 + [(lon, BF16)] * 2
    vmem, smem = pl.BlockSpec(memory_space=pltpu.VMEM), pl.BlockSpec(memory_space=pltpu.SMEM)
    anywhere = pl.BlockSpec(memory_space=pl.ANY)
    field_a, field_b, field_s, wet, rate, *sent = call(
        functools.partial(init_body, levels, columns),
        [(inner, F32), (outer, F32), (sides, F32), ((levels, columns, lat), F32), (row, F32)] + messages,
        2 * 10**6,
        in_specs=[smem] + [vmem] * 3 + [anywhere],
        scratch=[pltpu.VMEM(state.shape, F32), pltpu.SemaphoreType.DMA],
    )(rates, land_mask, wet_levels, state, basis)
    (gram,) = call(gram_body, [((1, 128), F32)], 2 * 10**6)(basis_rows)
    def fetched(part):
        return [part] + [shifted(part, "tracer", k) for k in range(1, n_tracer)]

    def prepared(pieces, n):
        return call(
            lambda *refs: prepare_body(refs[:-1], refs[-1], n),
            [((27, levels, columns, lat), F32)],
            2 * 10**6,
        )(*pieces)[0]

    inner_levels, outer_levels = list(range(1, levels - 1)), [0, levels - 1]
    steps = coefficients.shape[0] * n_month
    halos = shifted(sent[1], "month", 1), shifted(sent[0], "month", -1)
    groups = [[0], [1]] + ([list(range(2, steps))] if steps > 2 else [])
    pieces = [fetched(after(of_months(found, groups[0]), gram))]
    found = lax.optimization_barrier((found, halos))[0]
    pieces.append(fetched(of_months(found, groups[1])))
    for month in range(steps):
        group = min(month, 2)
        if month == 1 and len(groups) > 2:
            found = lax.optimization_barrier((found, left, right))[0]
            pieces.append(fetched(of_months(found, groups[2])))
        weights = prepared(pieces[group], month - groups[group][0])
        lev_lo, lev_hi, lon_lo, lon_hi = sent
        below, above = halos if month == 0 else (shifted(lev_hi, "month", 1), shifted(lev_lo, "month", -1))
        args = (weights, field_a, field_b, field_s, rate, wet)

        def part(mine, shape, is_outer, *more):
            return call(
                functools.partial(part_body, levels, columns, mine, is_outer),
                [(shape, F32)],
                10**7,
            )(*args, *more)[0]

        new_a = part(inner_levels, inner, False)
        left, right = call(
            functools.partial(pack_body, columns),
            [((2, levels + 2) + row, BF16)] * 2,
            10**5,
            in_specs=[anywhere] + [vmem] * 4,
        )(new_a if month else wet, below, above, lon_lo, lon_hi)
        left, right = shifted(right, "space", 1), shifted(left, "space", -1)
        new_b = part(outer_levels, outer, True, below, above)
        field_a, field_b = new_a, new_b
        ends = (new_a, new_b, weights, left, right, wet)
        if month < steps - 1:
            field_s, *sent = call(
                functools.partial(side_body, levels, columns), [(sides, F32)] + messages, 2 * 10**6,
            )(*ends)

    residual, product, tiles = call(
        functools.partial(last_body, levels, columns),
        [(state.shape, F32)] * 2 + [((n_space * n_tracer, 1, 128), F32)],
        4 * 10**6,
        scratch=[pltpu.VMEM(state.shape, F32)] * 2,
    )(*ends, state, basis, gram)

    def total(tiles):
        part = jnp.sum(spread(tiles, ("space", "tracer")), axis=0)
        return spread(copies(part, n_month), "month")

    cells = float(state.size * n_space * n_tracer * n_month)
    remainder, next_basis, krylov, sure = call(
        functools.partial(finish_body, cells), [(flat, F32)] * 2 + [((1, count + 2), F32), ((1, 1), F32)], 2 * 10**6
    )(total(tiles), product.reshape(flat), basis_rows)

    def direct(remainder, next_basis, krylov):
        own = jnp.broadcast_to(jnp.sum(remainder * remainder), (n_space * n_tracer, 1, 128))
        norm = jnp.sqrt(jnp.sum(total(own), axis=0)[0, 0] / cells + 1e-06)
        return remainder / norm, jnp.where(jnp.arange(count + 2) == count, norm, krylov)

    next_basis, krylov = lax.cond(
        sure[0, 0] > 0.5, lambda r, n, k: (n, k), direct, remainder, next_basis, krylov
    )
    return residual, next_basis.reshape(state.shape), krylov.reshape(count + 2)


def solution(mesh):
    return jax.shard_map(
        on_device,
        mesh=mesh,
        in_specs=(
            P("tracer", "month", "space", None),
            P("month", None, None, "space", None),
            P("tracer"),
            P("space", None),
            P("space", None),
            P(None, "tracer", "month", "space", None),
        ),
        out_specs=(P("tracer", "month", "space", None), P("tracer", "month", "space", None), P()),
        check_vma=False,
    )
```

```python
import functools

import jax
import jax.numpy as jnp
from jax import lax
from jax.experimental import pallas as pl
from jax.experimental.pallas import tpu as pltpu
from jax.sharding import PartitionSpec as P


F32 = jnp.float32
BF16 = jnp.bfloat16
TAPS = [(dl, di) for dl in (-1, 0, 1) for di in (-1, 0, 1)]


VMEM_LIMIT = 20 * 2**20


def call(body, outs, cost, scratch=(), in_specs=None):
    return pl.pallas_call(
        body,
        out_shape=[jax.ShapeDtypeStruct(s, d) for s, d in outs],
        scratch_shapes=list(scratch),
        cost_estimate=pl.CostEstimate(flops=cost, transcendentals=0, bytes_accessed=cost // 8),
        compiler_params=pltpu.CompilerParams(vmem_limit_bytes=VMEM_LIMIT),
        **({} if in_specs is None else {"in_specs": in_specs}),
    )


def keep_of(axis):
    place = lax.axis_index(axis)
    return [jnp.where(place > 0, 1.0, 0.0), jnp.where(place < lax.axis_size(axis) - 1, 1.0, 0.0)]


def reader(levels, columns, inner_ref, outer_ref, sides_ref):
    def get(f, l, i):
        if i in (0, columns - 1):
            return sides_ref[f, l, int(i > 0)]
        if l in (0, levels - 1):
            return outer_ref[f, int(l > 0), i]
        return inner_ref[f, l - 1, i]

    return get


def init_body(levels, columns, rates_ref, land_ref, depth_ref, state_ref, basis_ref, *outs):
    inner_ref, outer_ref, sides_ref, wet_ref, rate_ref, lev_lo, lev_hi, lon_lo, lon_hi, last_ref, sem = outs
    fetch = pltpu.make_async_copy(basis_ref.at[basis_ref.shape[0] - 1], last_ref, sem)
    fetch.start()
    tracer = lax.broadcasted_iota(jnp.int32, rate_ref.shape, 0)
    rate = jnp.zeros(rate_ref.shape, F32)
    for n in range(rate_ref.shape[0]):
        rate = jnp.where(tracer == n, rates_ref[n], rate)
    rate_ref[...] = rate
    for l in range(levels):
        ocean = (land_ref[...] == 1) & (lax.axis_index("month") * levels + l < depth_ref[...])
        wet_ref[l] = jnp.where(ocean, 1.0, 0.0).astype(F32)
    for f, ref in enumerate((state_ref, last_ref)):
        if f:
            fetch.wait()
        for l in range(levels):
            rows = pltpu.einshape("tix->itx", ref[:, l])
            for i in range(columns):
                row = rows[i] * wet_ref[l, pl.ds(i, 1), :]
                short = row.astype(BF16)
                if i in (0, columns - 1):
                    sides_ref[f, l, int(i > 0)] = row
                    (lon_hi if i else lon_lo)[f, l] = short
                elif l in (0, levels - 1):
                    outer_ref[f, int(l > 0), i] = row
                else:
                    inner_ref[f, l - 1, i] = row
                if l in (0, levels - 1):
                    (lev_hi if l else lev_lo)[f, i] = short


def combine(sums):
    n = sums[1].shape[1]
    return sums[1] + pltpu.roll(sums[2], n - 1, 1) + pltpu.roll(sums[0], 1, 1)


def tap_sums(taps):
    acc = [[None] * 3, [None] * 3]
    for weights, rows in taps:
        for dj in range(3):
            for f in range(2):
                term = weights[dj] * rows[f]
                acc[f][dj] = term if acc[f][dj] is None else acc[f][dj] + term
    return combine(acc[0]), combine(acc[1])


def prepare_body(month, months, *refs):
    sources, wf_ref = refs[:-1], refs[-1]
    n_parts = lax.axis_size("tracer")
    size = sources[0].shape[3]
    taps, levels, columns, lat = wf_ref.shape
    me = lax.axis_index("month")
    tests = [me == month] + [me < month] * (month > 0) + [me > month] * (month < months - 1)
    for n, test in enumerate(tests):

        @pl.when(test)
        def _(parts=sources[n * n_parts : (n + 1) * n_parts]):
            for n, ref in enumerate(parts):
                place = lax.rem(lax.axis_index("tracer") - n + n_parts, n_parts)
                lanes = pl.ds(pl.multiple_of(place * size, size), size)

                def spread_part(k, carry, ref=ref, lanes=lanes):
                    for l in range(levels):
                        wf_ref[k, l, :, lanes] = ref[k, l].astype(F32)
                    return carry

                lax.fori_loop(0, taps, spread_part, 0, unroll=3)

    lane = lax.broadcasted_iota(jnp.int32, (columns, lat), 1)

    def move(k, carry):
        for l in range(levels):
            wf_ref[3 * k + 2, l] = jnp.where(lane == 0, 0.0, pltpu.roll(wf_ref[3 * k + 2, l], 1, 1))
            wf_ref[3 * k, l] = jnp.where(lane == lat - 1, 0.0, pltpu.roll(wf_ref[3 * k, l], lat - 1, 1))
        return carry

    lax.fori_loop(0, taps // 3, move, 0, unroll=3)


def part_body(levels, columns, mine, outer, wf_ref, inner_ref, outer_ref, sides_ref, rate_ref, wet_ref, *rest):
    if outer:
        below_ref, above_ref, out_ref = rest
    else:
        (out_ref,) = rest
    get = reader(levels, columns, inner_ref, outer_ref, sides_ref)
    keep = keep_of("month")
    rate = rate_ref[...]

    def rows_at(l, i):
        if l < 0:
            return [below_ref[f, i].astype(F32) * keep[0] for f in range(2)]
        if l >= levels:
            return [above_ref[f, i].astype(F32) * keep[1] for f in range(2)]
        return [get(f, l, i) for f in range(2)]

    for n, l in enumerate(mine):
        for i in range(columns):
            taps = []
            for dl, di in TAPS:
                if 0 <= i + di < columns:
                    first = 9 * (dl + 1) + 3 * (di + 1)
                    weights = [wf_ref[first + dj, l, pl.ds(i, 1), :] for dj in range(3)]
                    taps.append((weights, rows_at(l + dl, i + di)))
            ac, at = tap_sums(taps)
            c, t = rows_at(l, i)
            square = c * c
            inverse = 1.0 / (1.0 + square)
            part = rate * square * inverse
            ac = ac - part * c
            at = at - part * inverse * (3.0 + square) * t
            if 0 < i < columns - 1:
                wet = wet_ref[l, pl.ds(i, 1), :]
                ac, at = ac * wet, at * wet
            out_ref[0, n, i] = ac
            out_ref[1, n, i] = at


def side_rows(levels, columns, inner_ref, outer_ref, wf_ref, left_ref, right_ref, wet_ref):
    keep_lev, keep_lon = keep_of("month"), keep_of("space")
    for l in range(levels):
        edge = l in (0, levels - 1)
        n = int(l > 0) if edge else l - 1
        own = outer_ref if edge else inner_ref
        for side, i in ((0, 0), (1, columns - 1)):
            halo = (left_ref, right_ref)[side]
            taps = []
            for d in range(3):
                keep = keep_lon[side]
                if not 0 <= l + d - 1 < levels:
                    keep = keep * keep_lev[int(l + d > levels)]
                weights = [wf_ref[9 * d + 6 * side + dj, l, pl.ds(i, 1), :] for dj in range(3)]
                taps.append((weights, [halo[f, l + d].astype(F32) * keep for f in range(2)]))
            sums = tap_sums(taps)
            wet = wet_ref[l, pl.ds(i, 1), :]
            yield l, side, i, [(own[f, n, i] + sums[f]) * wet for f in range(2)]


def side_body(levels, columns, *refs):
    sides_ref, lev_lo, lev_hi, lon_lo, lon_hi = refs[6:]
    outer_ref = refs[1]
    for l, side, i, rows in side_rows(levels, columns, *refs[:6]):
        for f in range(2):
            short = rows[f].astype(BF16)
            sides_ref[f, l, side] = rows[f]
            (lon_hi if side else lon_lo)[f, l] = short
            if l in (0, levels - 1):
                (lev_hi if l else lev_lo)[f, i] = short
    for f in range(2):
        for i in range(1, columns - 1):
            lev_lo[f, i] = outer_ref[f, 0, i].astype(BF16)
            lev_hi[f, i] = outer_ref[f, 1, i].astype(BF16)


def pack_body(columns, after_ref, below_ref, above_ref, lo_ref, hi_ref, left_out, right_out):
    levels = lo_ref.shape[1]
    for out, own, i in ((left_out, lo_ref, 0), (right_out, hi_ref, columns - 1)):
        for f in range(2):
            out[f, 0] = below_ref[f, i]
            out[f, levels + 1] = above_ref[f, i]
            for l in range(levels):
                out[f, l + 1] = own[f, l]


def lanes_of(values, first):
    lane = lax.broadcasted_iota(jnp.int32, (1, 128), 1)
    total = jnp.zeros((1, 128), F32)
    for n, v in enumerate(values):
        total = jnp.where(lane == first + n, v, total)
    return total


def gram_body(basis_ref, out_ref):
    count = basis_ref.shape[0]
    pairs = [(k, m) for k in range(count) for m in range(k, count)]

    def step(n, acc):
        rows = pl.ds(pl.multiple_of(n * 8, 8), 8)
        b = [basis_ref[k, rows, :] for k in range(count)]
        return tuple(a + b[k] * b[m] for a, (k, m) in zip(acc, pairs))

    zero = jnp.zeros((8, basis_ref.shape[2]), F32)
    acc = lax.fori_loop(0, basis_ref.shape[1] // 8, step, (zero,) * len(pairs))
    out_ref[...] = lanes_of([jnp.sum(a) for a in acc], 6)


def last_body(levels, columns, *refs):
    state_ref, basis_ref, gram_ref, res_ref, prod_ref, out_ref = refs[6:12]
    fields = refs[12:]
    inner_ref, outer_ref = refs[:2]
    sides = {}
    for l, side, i, rows in side_rows(levels, columns, *refs[:6]):
        sides[l, i] = rows
    for l in range(levels):
        for f in range(2):
            own = [sides[l, i][f] if i in (0, columns - 1)
                   else outer_ref[f, int(l > 0), i] if l in (0, levels - 1) else inner_ref[f, l - 1, i]
                   for i in range(columns)]
            fields[f][:, l] = pltpu.einshape("itx->tix", jnp.stack(own))
    count = basis_ref.shape[0]

    def step(n, acc):
        for l in range(levels):
            b = [basis_ref[k, n, l] for k in range(count)]
            residual = fields[0][n, l] - state_ref[n, l]
            product = fields[1][n, l] - b[count - 1]
            res_ref[n, l] = residual
            prod_ref[n, l] = product
            terms = [x * product for x in b] + [product * product, residual * residual]
            acc = tuple(a + x for a, x in zip(acc, terms))
        return acc

    zero = jnp.zeros(fields[0].shape[2:], F32)
    acc = lax.fori_loop(0, fields[0].shape[0], step, (zero,) * (count + 2))
    row = gram_ref[...] + lanes_of([jnp.sum(a) for a in acc], 0)
    for n in range(out_ref.shape[0]):
        out_ref[n] = row


def finish_body(cells, rows_ref, prod_ref, basis_ref, rem_ref, next_ref, krylov_ref, sure_ref):
    count = basis_ref.shape[0]
    means = rows_ref[0]
    for n in range(1, rows_ref.shape[0]):
        means = means + rows_ref[n]
    means = means / cells
    lane = lax.broadcasted_iota(jnp.int32, (1, 128), 1)

    def pick(n):
        return jnp.sum(jnp.where(lane == n, means, 0.0), axis=1, keepdims=True)

    coef = [pick(k) for k in range(count)]
    cross = sum(2.0 * c * c for c in coef)
    gram = 0.0
    place = count + 2
    for k in range(count):
        for m in range(k, count):
            gram = gram + (1.0 if k == m else 2.0) * coef[k] * coef[m] * pick(place)
            place += 1
    square = pick(count)
    expanded = square - cross + gram
    sure = jnp.where(expanded > 0.01 * (square + cross + gram), 1.0, 0.0)
    norm = jnp.sqrt(jnp.maximum(expanded, 0.0) + 1e-06)
    rms = jnp.sqrt(pick(count + 1) + 1e-06)
    krylov = jnp.where(lane == count, norm, jnp.where(lane == count + 1, rms, means))
    krylov_ref[...] = krylov[:, : count + 2]
    sure_ref[...] = sure
    inverse = 1.0 / norm

    def step(n, carry):
        rows = pl.ds(pl.multiple_of(n * 8, 8), 8)
        rem = coef[0] * basis_ref[0, rows, :]
        for k in range(1, count):
            rem = rem + coef[k] * basis_ref[k, rows, :]
        rem = prod_ref[rows, :] - rem
        rem_ref[rows, :] = rem
        next_ref[rows, :] = rem * inverse
        return carry

    lax.fori_loop(0, prod_ref.shape[0] // 8, step, 0)


def spread(x, axes):
    return lax.all_to_all(x, axes, 0, 0, tiled=True)


def copies(x, count):
    return jnp.broadcast_to(x[None], (count,) + x.shape)


def shifted(x, axis, by):
    size = lax.axis_size(axis)
    return lax.ppermute(x, axis, [(n, (n + by) % size) for n in range(size)])


def after(x, *others):
    return lax.optimization_barrier((x, *others))[0]


def extract_body(coef_ref, *refs):
    outs, sem = refs[:-1], refs[-1]
    levels, part = outs[0].shape[1], outs[0].shape[3]
    place = pl.ds(pl.multiple_of(lax.axis_index("tracer") * part, part), part)
    fetches = []
    for k, out in enumerate(outs):
        level = pl.ds(lax.rem(lax.axis_index("month") + k, len(outs)) * levels, levels)
        fetches.append(pltpu.make_async_copy(coef_ref.at[0, :, level, :, place], out, sem.at[k]))
        fetches[-1].start()
    for fetch in fetches:
        fetch.wait()


def month_parts(coefficients, levels):
    taps, _, columns, lat = coefficients.shape[1:]
    n_tracer, n_month = lax.axis_size("tracer"), lax.axis_size("month")
    own = call(
        extract_body,
        [((taps, levels, columns, lat // n_tracer), BF16)] * n_month,
        10**6,
        scratch=[pltpu.SemaphoreType.DMA((n_month,))],
        in_specs=[pl.BlockSpec(memory_space=pltpu.HBM)],
    )(pltpu.with_memory_space_constraint(coefficients, pltpu.HBM))
    return [own[0]] + [shifted(own[k], "month", k) for k in range(1, n_month)]


def select_body(turn, *refs):
    found, out = refs[:-1], refs[-1]
    me = lax.axis_index("month")
    month = jnp.where(turn < me, turn, turn + 1)
    place = lax.rem(me - month + len(found), len(found))
    for k, ref in enumerate(found):

        @pl.when(place == k)
        def _(ref=ref):
            out[...] = ref[...]


def of_turn(found, turn):
    return call(functools.partial(select_body, turn), [(found[0].shape, BF16)], 10**5)(*found)[0]


def one_step(state, coefficients, rates, land_mask, wet_levels, basis):
    tracers, levels, columns, lat = state.shape
    count = basis.shape[0]
    n_space, n_month, n_tracer = lax.axis_size("space"), lax.axis_size("month"), lax.axis_size("tracer")
    flat = (tracers * levels * columns, lat)
    basis_rows = basis.reshape((count,) + flat)
    found = month_parts(coefficients, levels)

    row = (tracers, lat)
    inner, outer = (2, levels - 2, columns) + row, (2, 2, columns) + row
    sides, lev, lon = (2, levels, 2) + row, (2, columns) + row, (2, levels) + row
    messages = [(lev, BF16)] * 2 + [(lon, BF16)] * 2
    vmem, smem = pl.BlockSpec(memory_space=pltpu.VMEM), pl.BlockSpec(memory_space=pltpu.SMEM)
    anywhere = pl.BlockSpec(memory_space=pl.ANY)
    field_a, field_b, field_s, wet, rate, *sent = call(
        functools.partial(init_body, levels, columns),
        [(inner, F32), (outer, F32), (sides, F32), ((levels, columns, lat), F32), (row, F32)] + messages,
        2 * 10**6,
        in_specs=[smem] + [vmem] * 3 + [anywhere],
        scratch=[pltpu.VMEM(state.shape, F32), pltpu.SemaphoreType.DMA],
    )(rates, land_mask, wet_levels, state, basis)
    (gram,) = call(gram_body, [((1, 128), F32)], 2 * 10**6)(basis_rows)

    def fetched(part):
        return [part] + [shifted(part, "tracer", k) for k in range(1, n_tracer)]

    def prepared(own, turns, month):
        sources = own + (turns[month - 1] if month else []) + (turns[month] if month < steps - 1 else [])
        return call(
            functools.partial(prepare_body, month, steps), [((27, levels, columns, lat), F32)], 2 * 10**6
        )(*sources)[0]

    inner_levels, outer_levels = list(range(1, levels - 1)), [0, levels - 1]
    steps = coefficients.shape[0] * n_month
    halos = shifted(sent[1], "month", 1), shifted(sent[0], "month", -1)
    own = fetched(found[0])
    turns = [fetched(after(of_turn(found, 0), gram))]
    found = lax.optimization_barrier((found, halos))[0]
    turns.append(fetched(of_turn(found, 1)))
    for month in range(steps):
        weights = prepared(own, turns, month) if month < 2 else next_weights
        lev_lo, lev_hi, lon_lo, lon_hi = sent
        below, above = halos if month == 0 else (shifted(lev_hi, "month", 1), shifted(lev_lo, "month", -1))
        args = (weights, field_a, field_b, field_s, rate, wet)

        def part(mine, shape, is_outer, *more):
            return call(
                functools.partial(part_body, levels, columns, mine, is_outer),
                [(shape, F32)],
                10**7,
            )(*args, *more)[0]

        new_a = part(inner_levels, inner, False)
        left, right = call(
            functools.partial(pack_body, columns),
            [((2, levels + 2) + row, BF16)] * 2,
            10**5,
            in_specs=[anywhere] + [vmem] * 4,
        )(new_a if month else wet, below, above, lon_lo, lon_hi)
        left, right = shifted(right, "space", 1), shifted(left, "space", -1)
        if month == 0:
            found = lax.optimization_barrier((found, left, right))[0]
            turns += [fetched(of_turn(found, turn)) for turn in range(2, steps - 1)]
        elif month < steps - 1:
            next_weights = prepared(own, turns, month + 1)
            left, right, next_weights = lax.optimization_barrier((left, right, next_weights))
        new_b = part(outer_levels, outer, True, below, above)
        field_a, field_b = new_a, new_b
        ends = (new_a, new_b, weights, left, right, wet)
        if month < steps - 1:
            field_s, *sent = call(
                functools.partial(side_body, levels, columns), [(sides, F32)] + messages, 2 * 10**6,
            )(*ends)

    residual, product, tiles = call(
        functools.partial(last_body, levels, columns),
        [(state.shape, F32)] * 2 + [((n_space * n_tracer, 1, 128), F32)],
        4 * 10**6,
        scratch=[pltpu.VMEM(state.shape, F32)] * 2,
    )(*ends, state, basis, gram)

    def total(tiles):
        part = jnp.sum(spread(tiles, ("space", "tracer")), axis=0)
        return spread(copies(part, n_month), "month")

    cells = float(state.size * n_space * n_tracer * n_month)
    remainder, next_basis, krylov, sure = call(
        functools.partial(finish_body, cells), [(flat, F32)] * 2 + [((1, count + 2), F32), ((1, 1), F32)], 2 * 10**6
    )(total(tiles), product.reshape(flat), basis_rows)

    def direct(remainder, next_basis, krylov):
        own = jnp.broadcast_to(jnp.sum(remainder * remainder), (n_space * n_tracer, 1, 128))
        norm = jnp.sqrt(jnp.sum(total(own), axis=0)[0, 0] / cells + 1e-06)
        return remainder / norm, jnp.where(jnp.arange(count + 2) == count, norm, krylov)

    next_basis, krylov = lax.cond(
        sure[0, 0] > 0.5, lambda r, n, k: (n, k), direct, remainder, next_basis, krylov
    )
    return residual, next_basis.reshape(state.shape), krylov.reshape(count + 2)


def solution(mesh):
    return jax.shard_map(
        one_step,
        mesh=mesh,
        in_specs=(
            P("tracer", "month", "space", None),
            P("month", None, None, "space", None),
            P("tracer"),
            P("space", None),
            P("space", None),
            P(None, "tracer", "month", "space", None),
        ),
        out_specs=(P("tracer", "month", "space", None), P("tracer", "month", "space", None), P()),
        check_vma=False,
    )
```

```python
import functools

import jax
import jax.numpy as jnp
from jax import lax
from jax.experimental import pallas as pl
from jax.experimental.pallas import tpu as pltpu
from jax.sharding import PartitionSpec as P


F32 = jnp.float32
BF16 = jnp.bfloat16
TAPS = [(dl, di) for dl in (-1, 0, 1) for di in (-1, 0, 1)]


VMEM_LIMIT = 20 * 2**20


def call(body, outs, cost, scratch=(), in_specs=None):
    return pl.pallas_call(
        body,
        out_shape=[jax.ShapeDtypeStruct(s, d) for s, d in outs],
        scratch_shapes=list(scratch),
        cost_estimate=pl.CostEstimate(flops=cost, transcendentals=0, bytes_accessed=cost // 8),
        compiler_params=pltpu.CompilerParams(vmem_limit_bytes=VMEM_LIMIT),
        **({} if in_specs is None else {"in_specs": in_specs}),
    )


def keep_of(axis):
    place = lax.axis_index(axis)
    return [jnp.where(place > 0, 1.0, 0.0), jnp.where(place < lax.axis_size(axis) - 1, 1.0, 0.0)]


def reader(levels, columns, inner_ref, outer_ref, sides_ref):
    def get(f, l, i):
        if i in (0, columns - 1):
            return sides_ref[f, l, int(i > 0)]
        if l in (0, levels - 1):
            return outer_ref[f, int(l > 0), i]
        return inner_ref[f, l - 1, i]

    return get


def init_body(levels, columns, rates_ref, land_ref, depth_ref, state_ref, basis_ref, *outs):
    inner_ref, outer_ref, sides_ref, wet_ref, rate_ref, lev_lo, lev_hi, lon_lo, lon_hi, last_ref, sem = outs
    fetch = pltpu.make_async_copy(basis_ref.at[basis_ref.shape[0] - 1], last_ref, sem)
    fetch.start()
    tracer = lax.broadcasted_iota(jnp.int32, rate_ref.shape, 0)
    rate = jnp.zeros(rate_ref.shape, F32)
    for n in range(rate_ref.shape[0]):
        rate = jnp.where(tracer == n, rates_ref[n], rate)
    rate_ref[...] = rate
    for l in range(levels):
        ocean = (land_ref[...] == 1) & (lax.axis_index("month") * levels + l < depth_ref[...])
        wet_ref[l] = jnp.where(ocean, 1.0, 0.0).astype(F32)
    for f, ref in enumerate((state_ref, last_ref)):
        if f:
            fetch.wait()
        for l in range(levels):
            rows = pltpu.einshape("tix->itx", ref[:, l])
            for i in range(columns):
                row = rows[i] * wet_ref[l, pl.ds(i, 1), :]
                short = row.astype(BF16)
                if i in (0, columns - 1):
                    sides_ref[f, l, int(i > 0)] = row
                    (lon_hi if i else lon_lo)[f, l] = short
                elif l in (0, levels - 1):
                    outer_ref[f, int(l > 0), i] = row
                else:
                    inner_ref[f, l - 1, i] = row
                if l in (0, levels - 1):
                    (lev_hi if l else lev_lo)[f, i] = short


def combine(sums):
    n = sums[1].shape[1]
    return sums[1] + pltpu.roll(sums[2], n - 1, 1) + pltpu.roll(sums[0], 1, 1)


def tap_sums(taps):
    acc = [[None] * 3, [None] * 3]
    for weights, rows in taps:
        for dj in range(3):
            for f in range(2):
                term = weights[dj] * rows[f]
                acc[f][dj] = term if acc[f][dj] is None else acc[f][dj] + term
    return combine(acc[0]), combine(acc[1])


def prepare_body(month, months, *refs):
    sources, wf_ref = refs[:-1], refs[-1]
    n_parts = lax.axis_size("tracer")
    size = sources[0].shape[3]
    taps, levels, columns, lat = wf_ref.shape
    me = lax.axis_index("month")
    tests = [me == month] + [me < month] * (month > 0) + [me > month] * (month < months - 1)
    for n, test in enumerate(tests):

        @pl.when(test)
        def _(parts=sources[n * n_parts : (n + 1) * n_parts]):
            for n, ref in enumerate(parts):
                place = lax.rem(lax.axis_index("tracer") - n + n_parts, n_parts)
                lanes = pl.ds(pl.multiple_of(place * size, size), size)

                def spread_part(k, carry, ref=ref, lanes=lanes):
                    for l in range(levels):
                        wf_ref[k, l, :, lanes] = ref[k, l].astype(F32)
                    return carry

                lax.fori_loop(0, taps, spread_part, 0, unroll=3)

    lane = lax.broadcasted_iota(jnp.int32, (columns, lat), 1)

    def move(k, carry):
        for l in range(levels):
            wf_ref[3 * k + 2, l] = jnp.where(lane == 0, 0.0, pltpu.roll(wf_ref[3 * k + 2, l], 1, 1))
            wf_ref[3 * k, l] = jnp.where(lane == lat - 1, 0.0, pltpu.roll(wf_ref[3 * k, l], lat - 1, 1))
        return carry

    lax.fori_loop(0, taps // 3, move, 0, unroll=3)


def part_body(levels, columns, mine, outer, wf_ref, inner_ref, outer_ref, sides_ref, rate_ref, wet_ref, *rest):
    if outer:
        below_ref, above_ref, out_ref = rest
    else:
        (out_ref,) = rest
    get = reader(levels, columns, inner_ref, outer_ref, sides_ref)
    keep = keep_of("month")
    rate = rate_ref[...]

    def rows_at(l, i):
        if l < 0:
            return [below_ref[f, i].astype(F32) * keep[0] for f in range(2)]
        if l >= levels:
            return [above_ref[f, i].astype(F32) * keep[1] for f in range(2)]
        return [get(f, l, i) for f in range(2)]

    for n, l in enumerate(mine):
        for i in range(columns):
            taps = []
            for dl, di in TAPS:
                if 0 <= i + di < columns:
                    first = 9 * (dl + 1) + 3 * (di + 1)
                    weights = [wf_ref[first + dj, l, pl.ds(i, 1), :] for dj in range(3)]
                    taps.append((weights, rows_at(l + dl, i + di)))
            ac, at = tap_sums(taps)
            c, t = rows_at(l, i)
            square = c * c
            inverse = 1.0 / (1.0 + square)
            part = rate * square * inverse
            ac = ac - part * c
            at = at - part * inverse * (3.0 + square) * t
            if 0 < i < columns - 1:
                wet = wet_ref[l, pl.ds(i, 1), :]
                ac, at = ac * wet, at * wet
            out_ref[0, n, i] = ac
            out_ref[1, n, i] = at


def side_rows(levels, columns, inner_ref, outer_ref, wf_ref, left_ref, right_ref, wet_ref):
    keep_lev, keep_lon = keep_of("month"), keep_of("space")
    for l in range(levels):
        edge = l in (0, levels - 1)
        n = int(l > 0) if edge else l - 1
        own = outer_ref if edge else inner_ref
        for side, i in ((0, 0), (1, columns - 1)):
            halo = (left_ref, right_ref)[side]
            taps = []
            for d in range(3):
                keep = keep_lon[side]
                if not 0 <= l + d - 1 < levels:
                    keep = keep * keep_lev[int(l + d > levels)]
                weights = [wf_ref[9 * d + 6 * side + dj, l, pl.ds(i, 1), :] for dj in range(3)]
                taps.append((weights, [halo[f, l + d].astype(F32) * keep for f in range(2)]))
            sums = tap_sums(taps)
            wet = wet_ref[l, pl.ds(i, 1), :]
            yield l, side, i, [(own[f, n, i] + sums[f]) * wet for f in range(2)]


def side_body(levels, columns, *refs):
    sides_ref, lev_lo, lev_hi, lon_lo, lon_hi = refs[6:]
    outer_ref = refs[1]
    for l, side, i, rows in side_rows(levels, columns, *refs[:6]):
        for f in range(2):
            short = rows[f].astype(BF16)
            sides_ref[f, l, side] = rows[f]
            (lon_hi if side else lon_lo)[f, l] = short
            if l in (0, levels - 1):
                (lev_hi if l else lev_lo)[f, i] = short
    for f in range(2):
        for i in range(1, columns - 1):
            lev_lo[f, i] = outer_ref[f, 0, i].astype(BF16)
            lev_hi[f, i] = outer_ref[f, 1, i].astype(BF16)


def pack_body(columns, after_ref, below_ref, above_ref, lo_ref, hi_ref, left_out, right_out):
    levels = lo_ref.shape[1]
    for out, own, i in ((left_out, lo_ref, 0), (right_out, hi_ref, columns - 1)):
        for f in range(2):
            out[f, 0] = below_ref[f, i]
            out[f, levels + 1] = above_ref[f, i]
            for l in range(levels):
                out[f, l + 1] = own[f, l]


def lanes_of(values, first):
    lane = lax.broadcasted_iota(jnp.int32, (1, 128), 1)
    total = jnp.zeros((1, 128), F32)
    for n, v in enumerate(values):
        total = jnp.where(lane == first + n, v, total)
    return total


def gram_body(basis_ref, out_ref):
    count = basis_ref.shape[0]
    pairs = [(k, m) for k in range(count) for m in range(k, count)]

    def step(n, acc):
        rows = pl.ds(pl.multiple_of(n * 8, 8), 8)
        b = [basis_ref[k, rows, :] for k in range(count)]
        return tuple(a + b[k] * b[m] for a, (k, m) in zip(acc, pairs))

    zero = jnp.zeros((8, basis_ref.shape[2]), F32)
    acc = lax.fori_loop(0, basis_ref.shape[1] // 8, step, (zero,) * len(pairs))
    out_ref[...] = lanes_of([jnp.sum(a) for a in acc], 6)


def last_body(levels, columns, *refs):
    state_ref, basis_ref, gram_ref, res_ref, prod_ref, out_ref = refs[6:12]
    fields = refs[12:]
    inner_ref, outer_ref = refs[:2]
    sides = {}
    for l, side, i, rows in side_rows(levels, columns, *refs[:6]):
        sides[l, i] = rows
    for l in range(levels):
        for f in range(2):
            own = [sides[l, i][f] if i in (0, columns - 1)
                   else outer_ref[f, int(l > 0), i] if l in (0, levels - 1) else inner_ref[f, l - 1, i]
                   for i in range(columns)]
            fields[f][:, l] = pltpu.einshape("itx->tix", jnp.stack(own))
    count = basis_ref.shape[0]

    def step(n, acc):
        for l in range(levels):
            b = [basis_ref[k, n, l] for k in range(count)]
            residual = fields[0][n, l] - state_ref[n, l]
            product = fields[1][n, l] - b[count - 1]
            res_ref[n, l] = residual
            prod_ref[n, l] = product
            terms = [x * product for x in b] + [product * product, residual * residual]
            acc = tuple(a + x for a, x in zip(acc, terms))
        return acc

    zero = jnp.zeros(fields[0].shape[2:], F32)
    acc = lax.fori_loop(0, fields[0].shape[0], step, (zero,) * (count + 2))
    row = gram_ref[...] + lanes_of([jnp.sum(a) for a in acc], 0)
    for n in range(out_ref.shape[0]):
        out_ref[n] = row


def finish_body(cells, rows_ref, prod_ref, basis_ref, rem_ref, next_ref, krylov_ref, sure_ref):
    count = basis_ref.shape[0]
    means = rows_ref[0]
    for n in range(1, rows_ref.shape[0]):
        means = means + rows_ref[n]
    means = means / cells
    lane = lax.broadcasted_iota(jnp.int32, (1, 128), 1)

    def pick(n):
        return jnp.sum(jnp.where(lane == n, means, 0.0), axis=1, keepdims=True)

    coef = [pick(k) for k in range(count)]
    cross = sum(2.0 * c * c for c in coef)
    gram = 0.0
    place = count + 2
    for k in range(count):
        for m in range(k, count):
            gram = gram + (1.0 if k == m else 2.0) * coef[k] * coef[m] * pick(place)
            place += 1
    square = pick(count)
    expanded = square - cross + gram
    sure = jnp.where(expanded > 0.01 * (square + cross + gram), 1.0, 0.0)
    norm = jnp.sqrt(jnp.maximum(expanded, 0.0) + 1e-06)
    rms = jnp.sqrt(pick(count + 1) + 1e-06)
    krylov = jnp.where(lane == count, norm, jnp.where(lane == count + 1, rms, means))
    krylov_ref[...] = krylov[:, : count + 2]
    sure_ref[...] = sure
    inverse = 1.0 / norm

    def step(n, carry):
        rows = pl.ds(pl.multiple_of(n * 8, 8), 8)
        rem = coef[0] * basis_ref[0, rows, :]
        for k in range(1, count):
            rem = rem + coef[k] * basis_ref[k, rows, :]
        rem = prod_ref[rows, :] - rem
        rem_ref[rows, :] = rem
        next_ref[rows, :] = rem * inverse
        return carry

    lax.fori_loop(0, prod_ref.shape[0] // 8, step, 0)


def spread(x, axes):
    return lax.all_to_all(x, axes, 0, 0, tiled=True)


def copies(x, count):
    return jnp.broadcast_to(x[None], (count,) + x.shape)


def shifted(x, axis, by):
    size = lax.axis_size(axis)
    return lax.ppermute(x, axis, [(n, (n + by) % size) for n in range(size)])


def after(x, *others):
    return lax.optimization_barrier((x, *others))[0]


def extract_body(coef_ref, *refs):
    outs, sem = refs[:-1], refs[-1]
    levels, part = outs[0].shape[1], outs[0].shape[3]
    place = pl.ds(pl.multiple_of(lax.axis_index("tracer") * part, part), part)
    fetches = []
    for k, out in enumerate(outs):
        level = pl.ds(lax.rem(lax.axis_index("month") + k, len(outs)) * levels, levels)
        fetches.append(pltpu.make_async_copy(coef_ref.at[0, :, level, :, place], out, sem.at[k]))
        fetches[-1].start()
    for fetch in fetches:
        fetch.wait()


def month_parts(coefficients, levels):
    taps, _, columns, lat = coefficients.shape[1:]
    n_tracer, n_month = lax.axis_size("tracer"), lax.axis_size("month")
    own = call(
        extract_body,
        [((taps, levels, columns, lat // n_tracer), BF16)] * n_month,
        10**6,
        scratch=[pltpu.SemaphoreType.DMA((n_month,))],
        in_specs=[pl.BlockSpec(memory_space=pltpu.HBM)],
    )(pltpu.with_memory_space_constraint(coefficients, pltpu.HBM))
    return [own[0]] + [shifted(own[k], "month", k) for k in range(1, n_month)]


def select_body(turn, *refs):
    found, out = refs[:-1], refs[-1]
    me = lax.axis_index("month")
    month = jnp.where(turn < me, turn, turn + 1)
    place = lax.rem(me - month + len(found), len(found))
    for k, ref in enumerate(found):

        @pl.when(place == k)
        def _(ref=ref):
            out[...] = ref[...]


def of_turn(found, turn):
    return call(functools.partial(select_body, turn), [(found[0].shape, BF16)], 10**5)(*found)[0]


def one_step(state, coefficients, rates, land_mask, wet_levels, basis):
    tracers, levels, columns, lat = state.shape
    count = basis.shape[0]
    n_space, n_month, n_tracer = lax.axis_size("space"), lax.axis_size("month"), lax.axis_size("tracer")
    flat = (tracers * levels * columns, lat)
    basis_rows = basis.reshape((count,) + flat)
    found = month_parts(coefficients, levels)

    row = (tracers, lat)
    inner, outer = (2, levels - 2, columns) + row, (2, 2, columns) + row
    sides, lev, lon = (2, levels, 2) + row, (2, columns) + row, (2, levels) + row
    messages = [(lev, BF16)] * 2 + [(lon, BF16)] * 2
    vmem, smem = pl.BlockSpec(memory_space=pltpu.VMEM), pl.BlockSpec(memory_space=pltpu.SMEM)
    anywhere = pl.BlockSpec(memory_space=pl.ANY)
    field_a, field_b, field_s, wet, rate, *sent = call(
        functools.partial(init_body, levels, columns),
        [(inner, F32), (outer, F32), (sides, F32), ((levels, columns, lat), F32), (row, F32)] + messages,
        2 * 10**6,
        in_specs=[smem] + [vmem] * 3 + [anywhere],
        scratch=[pltpu.VMEM(state.shape, F32), pltpu.SemaphoreType.DMA],
    )(rates, land_mask, wet_levels, state, basis)
    (gram,) = call(gram_body, [((1, 128), F32)], 2 * 10**6)(basis_rows)

    def fetched(part):
        return [part] + [shifted(part, "tracer", k) for k in range(1, n_tracer)]

    def prepared(own, turns, month):
        sources = own + (turns[month - 1] if month else []) + (turns[month] if month < steps - 1 else [])
        return call(
            functools.partial(prepare_body, month, steps), [((27, levels, columns, lat), F32)], 2 * 10**6
        )(*sources)[0]

    inner_levels, outer_levels = list(range(1, levels - 1)), [0, levels - 1]
    steps = coefficients.shape[0] * n_month
    halos = shifted(sent[1], "month", 1), shifted(sent[0], "month", -1)
    own = fetched(found[0])
    turns = [fetched(after(of_turn(found, 0), gram))]
    found = lax.optimization_barrier((found, halos))[0]
    turns.append(fetched(of_turn(found, 1)))
    turns += [fetched(of_turn(found, turn)) for turn in range(2, steps - 1)]
    for month in range(steps):
        if month < 2:
            weights = prepared(own, turns, month)
        else:
            weights = next_weights
        lev_lo, lev_hi, lon_lo, lon_hi = sent
        below, above = halos if month == 0 else (shifted(lev_hi, "month", 1), shifted(lev_lo, "month", -1))
        args = (weights, field_a, field_b, field_s, rate, wet)

        def part(mine, shape, is_outer, *more):
            return call(
                functools.partial(part_body, levels, columns, mine, is_outer),
                [(shape, F32)],
                10**7,
            )(*args, *more)[0]

        new_a = part(inner_levels, inner, False)
        left, right = call(
            functools.partial(pack_body, columns),
            [((2, levels + 2) + row, BF16)] * 2,
            10**5,
            in_specs=[anywhere] + [vmem] * 4,
        )(new_a if month else wet, below, above, lon_lo, lon_hi)
        left, right = shifted(right, "space", 1), shifted(left, "space", -1)
        if 0 < month < steps - 1:
            next_weights = prepared(own, turns, month + 1)
            left, right, next_weights = lax.optimization_barrier((left, right, next_weights))
        new_b = part(outer_levels, outer, True, below, above)
        field_a, field_b = new_a, new_b
        ends = (new_a, new_b, weights, left, right, wet)
        if month < steps - 1:
            field_s, *sent = call(
                functools.partial(side_body, levels, columns), [(sides, F32)] + messages, 2 * 10**6,
            )(*ends)

    residual, product, tiles = call(
        functools.partial(last_body, levels, columns),
        [(state.shape, F32)] * 2 + [((n_space * n_tracer, 1, 128), F32)],
        4 * 10**6,
        scratch=[pltpu.VMEM(state.shape, F32)] * 2,
    )(*ends, state, basis, gram)

    def total(tiles):
        part = jnp.sum(spread(tiles, ("space", "tracer")), axis=0)
        return spread(copies(part, n_month), "month")

    cells = float(state.size * n_space * n_tracer * n_month)
    remainder, next_basis, krylov, sure = call(
        functools.partial(finish_body, cells), [(flat, F32)] * 2 + [((1, count + 2), F32), ((1, 1), F32)], 2 * 10**6
    )(total(tiles), product.reshape(flat), basis_rows)

    def direct(remainder, next_basis, krylov):
        own = jnp.broadcast_to(jnp.sum(remainder * remainder), (n_space * n_tracer, 1, 128))
        norm = jnp.sqrt(jnp.sum(total(own), axis=0)[0, 0] / cells + 1e-06)
        return remainder / norm, jnp.where(jnp.arange(count + 2) == count, norm, krylov)

    next_basis, krylov = lax.cond(
        sure[0, 0] > 0.5, lambda r, n, k: (n, k), direct, remainder, next_basis, krylov
    )
    return residual, next_basis.reshape(state.shape), krylov.reshape(count + 2)


def solution(mesh):
    return jax.shard_map(
        one_step,
        mesh=mesh,
        in_specs=(
            P("tracer", "month", "space", None),
            P("month", None, None, "space", None),
            P("tracer"),
            P("space", None),
            P("space", None),
            P(None, "tracer", "month", "space", None),
        ),
        out_specs=(P("tracer", "month", "space", None), P("tracer", "month", "space", None), P()),
        check_vma=False,
    )
```
